32 devices in a mesh: gx: 4 (over y, core), gy: 8 (over z, x).
Axes of the slice: x: 2, y: 2, z: 4, core: 2. Of those that a mesh axis runs over, the one named last changes fastest.
Arguments:
- displacement: float32 [3, 32, 64, 128], P(None, 'gx', 'gy'), may hold values from -0.12 to 0.12
- velocity: float32 [3, 32, 64, 128], P(None, 'gx', 'gy'), may hold values from -4 to 4
- intact: int32 [61, 32, 64, 128], P(None, 'gx', 'gy'), may hold values 0 or 1
- material: int32 [32, 64, 128], P('gx', 'gy'), may hold values from 0 to 7
- bulk_modulus: float32 [8], replicated, may hold values from 80 to 800
- shear_modulus: float32 [8], replicated, may hold values from 40 to 400
- density: float32 [8], replicated, may hold values from 1 to 4
Outputs:
- new_displacement: float32 [3, 32, 64, 128], P(None, 'gx', 'gy')
- new_velocity: float32 [3, 32, 64, 128], P(None, 'gx', 'gy')
- last_force: float32 [3, 32, 64, 128], P(None, 'gx', 'gy')
The draws below stay inside these ranges and needn't reach their ends.
Inputs may be any that keep to these rules, and one draw needn't show every extreme that they name: intact[k, i] refers to the bond from node i to node i + e_k.
All inputs are finite; a program needn't handle non-finite values. No bound on the sum of `intact` on one device may be relied on, other than what follows from the above.
Results may differ from the reference program's by a relative error of at most 0.00002.
Values sent between devices are 32-bit elements; how exact they have to be, the bound alone decides.
A program may use at most 64 MiB of HBM per device.

```python
import math
import jax
import jax.numpy as jnp

NZ = 128
STEPS = 2
BONDS = 61
CLASSES = 8
NX = 32
NY = 64


def set_ends(values, own_key, smallest, largest):
    index_at = [jax.random.randint(jax.random.fold_in(own_key, axis), (), 0, length) for axis, length in enumerate(values.shape)]
    main_axis = values.shape.index(max(values.shape))
    next_to = index_at[:main_axis] + [(index_at[main_axis] + 1) % values.shape[main_axis]] + index_at[main_axis + 1:]
    return values.at[tuple(index_at)].set(smallest).at[tuple(next_to)].set(largest)


def block_scale(stream_key, shape, shards, least, largest):
    level = 1.0
    for dim, blocks in shards:
        steps = jax.random.uniform(jax.random.fold_in(jax.random.fold_in(stream_key, 6), dim), (blocks,), jnp.float32, least / len(shards), largest / len(shards))
        level = level * jnp.repeat(jnp.exp(steps), shape[dim] // blocks).reshape((-1,) + (1,) * (len(shape) - 1 - dim))
    return level


def centred(key, dims, deviation, limit, pieces=(), kind=jnp.bfloat16):
    entries = jax.random.normal(key, dims, jnp.float32) * deviation
    if len(pieces) > 0:
        entries = block_scale(key, dims, pieces, -0.22, 0.18) * entries
    return jnp.clip(entries, min=-limit, max=limit).astype(kind)


def setup_inputs(seed: int = 0) -> dict:
    keys = jax.random.split(jax.random.key(seed), 8)
    displacement = centred(keys[0], (3, NX, NY, NZ), 0.03, 0.12, ((1, 4), (2, 8)), jnp.float32)
    velocity = centred(keys[1], (3, NX, NY, NZ), 1.0, 4.0, ((1, 4), (2, 8)), jnp.float32)
    intact = set_ends((jax.random.randint(keys[2], (BONDS, NX, NY, NZ), 0, 8) < 7).astype(jnp.int32), jax.random.fold_in(keys[2], 1), 0, 1)
    material = set_ends(jax.random.randint(keys[3], (NX, NY, NZ), 0, CLASSES), jax.random.fold_in(keys[3], 1), 0, CLASSES - 1).astype(jnp.int32)
    bulk_modulus = jnp.clip(jnp.exp(jax.random.uniform(keys[4], (CLASSES,), jnp.float32, math.log(80.0), math.log(800.0))), 80.0, 800.0)
    shear_modulus = jnp.clip(jnp.exp(jax.random.uniform(keys[5], (CLASSES,), jnp.float32, math.log(40.0), math.log(400.0))), 40.0, 400.0)
    density = jnp.clip(jnp.exp(jax.random.uniform(keys[6], (CLASSES,), jnp.float32, math.log(1.0), math.log(4.0))), 1.0, 4.0)
    return dict(displacement=displacement, velocity=velocity, intact=intact, material=material, bulk_modulus=bulk_modulus, shear_modulus=shear_modulus, density=density)


time_step = 0.02

def half_offsets():
    result = []
    for along_x in range(-3, 4):
        for along_y in range(-3, 4):
            for along_z in range(-3, 4):
                if along_x * along_x + along_y * along_y + along_z * along_z <= 9 and (along_x, along_y, along_z) > (0, 0, 0):
                    result.append((along_x, along_y, along_z))
    return result

def weighted_volume(offsets):
    return 2.0 * sum((math.sqrt(float(offset[0] * offset[0] + offset[1] * offset[1] + offset[2] * offset[2])) for offset in offsets))

def neighbour(padded, offset, extent):
    return padded[..., 3 + offset[0]:3 + offset[0] + extent[0], 3 + offset[1]:3 + offset[1] + extent[1], 3 + offset[2]:3 + offset[2] + extent[2]]

def stretch_terms(motion, padded_motion, offset, extent):
    partner = neighbour(padded_motion, offset, extent)
    radius = math.sqrt(float(offset[0] * offset[0] + offset[1] * offset[1] + offset[2] * offset[2]))
    components = [offset[number] + partner[number] - motion[number] for number in range(3)]
    length = jnp.sqrt(components[0] * components[0] + components[1] * components[1] + components[2] * components[2])
    return (components, length, length - radius, radius)

def node_force(motion, bulk_node, shear_node, intact, inside, offsets, volume):
    extent = bulk_node.shape
    padded_motion = jnp.pad(motion, ((0, 0), (3, 3), (3, 3), (3, 3)))
    own_sum = jnp.zeros(extent, jnp.float32)
    gathered = jnp.zeros(inside.shape, jnp.float32)
    for bond_index, offset in enumerate(offsets):
        components, length, stretch, radius = stretch_terms(motion, padded_motion, offset, extent)
        weight = intact[bond_index].astype(jnp.float32) * neighbour(inside, offset, extent)
        contribution = weight * stretch
        own_sum = own_sum + contribution
        gathered = gathered.at[3 + offset[0]:3 + offset[0] + extent[0], 3 + offset[1]:3 + offset[1] + extent[1], 3 + offset[2]:3 + offset[2] + extent[2]].add(contribution)
    dilatation = 3.0 / volume * (own_sum + gathered[3:-3, 3:-3, 3:-3])
    pressure = jnp.pad(bulk_node * dilatation, 3)
    shear_padded = jnp.pad(shear_node, 3)
    twisting = jnp.pad(shear_node * dilatation, 3)
    own_force = jnp.zeros(motion.shape, jnp.float32)
    returned = jnp.zeros(padded_motion.shape, jnp.float32)
    for bond_index, offset in enumerate(offsets):
        components, length, stretch, radius = stretch_terms(motion, padded_motion, offset, extent)
        weight = intact[bond_index].astype(jnp.float32) * neighbour(inside, offset, extent)
        tension = weight / radius * (3.0 * radius / volume * (bulk_node * dilatation + neighbour(pressure, offset, extent)) + 15.0 / volume * ((shear_node + neighbour(shear_padded, offset, extent)) * stretch - radius / 3.0 * (shear_node * dilatation + neighbour(twisting, offset, extent))))
        vector = jnp.stack([tension * component / length for component in components])
        own_force = own_force + vector
        returned = returned.at[:, 3 + offset[0]:3 + offset[0] + extent[0], 3 + offset[1]:3 + offset[1] + extent[1], 3 + offset[2]:3 + offset[2] + extent[2]].add(vector)
    return own_force - returned[:, 3:-3, 3:-3, 3:-3]

def reference(displacement, velocity, intact, material, bulk_modulus, shear_modulus, density):
    offsets = half_offsets()
    volume = weighted_volume(offsets)
    bulk_node = bulk_modulus[material]
    shear_node = shear_modulus[material]
    inertia = density[material]
    inside = jnp.pad(jnp.ones(material.shape, jnp.float32), 3)
    forces = jnp.zeros(displacement.shape, jnp.float32)
    for counter in range(STEPS):
        forces = node_force(displacement, bulk_node, shear_node, intact, inside, offsets, volume)
        velocity = velocity + time_step * forces / inertia
        displacement = displacement + time_step * velocity
    return (displacement, velocity, forces)
```

```python
import functools
import math

import jax
import jax.numpy as jnp
from jax import lax
from jax.experimental import pallas as pl
from jax.experimental.pallas import tpu as pltpu
from jax.sharding import PartitionSpec as P

STEPS = 2
TIME_STEP = 0.02
REACH = 3
NEAR = 2
MESH = pl.DeviceIdType.MESH
F32 = jnp.float32

AROUND = [(dx, dy) for dx in (-1, 0, 1) for dy in (-1, 0, 1) if (dx, dy) != (0, 0)]
STATE = [("S", (-1, 0)), ("S", (0, -1)), ("S", (0, 1)), ("S", (-1, -1)), ("S", (-1, 1))]
CHUNKS = {
    "C": [("C", (1, -1)), ("C", (1, 1)), ("C", (0, -1)), ("C", (0, 1)), ("C", (1, 0))],
    "A": [("A", (-1, -1)), ("A", (-1, 1)), ("A", (0, -1)), ("A", (0, 1)), ("A", (-1, 0))],
    "B": [("B", (0, -1)), ("B", (0, 1))],
}
FINAL = {
    "C": [("C", (1, -1)), ("C", (1, 1)), ("C", (1, 0))],
    "A": [("A", (0, -1)), ("A", (0, 1))],
    "B": [("B", (0, -1)), ("B", (0, 1))],
}
SLOT = {key: n for n, key in enumerate(CHUNKS["C"] + CHUNKS["A"] + CHUNKS["B"])}
SLOT.update({key: n for n, key in enumerate(STATE)})


def half_offsets():
    span = range(-REACH, REACH + 1)
    return [
        (a, b, c)
        for a in span
        for b in span
        for c in span
        if a * a + b * b + c * c <= REACH * REACH and (a, b, c) > (0, 0, 0)
    ]


OFFSETS = half_offsets()
GROUPS = {}
for _k, (_a, _b, _c) in enumerate(OFFSETS):
    GROUPS.setdefault((_a, _b), []).append((_k, _c))
RADII = [math.sqrt(float(a * a + b * b + c * c)) for a, b, c in OFFSETS]
VOLUME = 2.0 * sum(RADII)


def round_up(value, unit):
    return -(-value // unit) * unit


def spans(rows, cols, key, kind):
    chunk, (dx, dy) = key
    own = {(r, c) for r in range(rows) for c in range(cols)}
    wide = own | {(r + a, c + b) for r, c in own for a, b in GROUPS}
    sender = own if kind == "state" else wide
    receiver = own if kind == "final" else wide
    first, end = {
        "A": (0, REACH), "B": (REACH, rows), "C": (rows, rows + REACH), "S": (0, rows)
    }[chunk]
    runs = []
    for row in range(first, end):
        used = [c for r, c in sender if r == row and (r - dx * rows, c - dy * cols) in receiver]
        if used:
            runs.append((row, min(used), max(used) + 1 - min(used)))
    return runs


def stages():
    listed = [("u", "state", 3), ("m", "state", 1), ("v", "state", 3)]
    for step in range(STEPS):
        listed.append((("t", step), "sum", 1))
        listed.append((("f", step), "final" if step == STEPS - 1 else "sum", 3))
    return listed


def keys_of(kind):
    if kind == "state":
        return STATE
    chunks = FINAL if kind == "final" else CHUNKS
    return chunks["C"] + chunks["A"] + chunks["B"]


def layout(rows, cols):
    place, at = {}, 0
    for number, (_, kind, comps) in enumerate(stages()):
        for key in keys_of(kind):
            if key[1][1] == 0:
                continue
            runs = spans(rows, cols, key, kind)
            size = round_up(comps * sum(width for _, _, width in runs), 8)
            place[number, key] = (at, size, runs)
            at += size
    return place, at


def tree_sum(terms):
    while len(terms) > 1:
        terms = [
            terms[n] + terms[n + 1] if n + 1 < len(terms) else terms[n]
            for n in range(0, len(terms), 2)
        ]
    return terms[0]


def kernel(
    grid_rows,
    grid_cols,
    u_hbm,
    v_hbm,
    intact_hbm,
    mat_hbm,
    bulk_hbm,
    shear_hbm,
    dens_hbm,
    out_u,
    out_v,
    out_f,
    u_ref,
    v_ref,
    mat_ref,
    mat_f32,
    bulk_ref,
    shear_ref,
    dens_ref,
    intact_ref,
    flag,
    by_inverse,
    by_stretch,
    wide_u,
    wide_v,
    wide_m,
    u_shift,
    a_shift,
    b_shift,
    a_coef,
    inertia,
    strain,
    force,
    send_buf,
    recv_buf,
    u_slab,
    m_slab,
    v_slab,
    t_slab,
    f_slab,
    local_sem,
    send_sem,
    recv_sem,
):
    rows, cols, nz = mat_ref.shape
    wide_rows = rows + REACH
    gx = lax.axis_index("gx")
    gy = lax.axis_index("gy")
    place, _ = layout(rows, cols)
    listed = stages()
    number_of = {name: number for number, (name, _, _) in enumerate(listed)}

    def present(direction):
        x = gx + direction[0]
        y = gy + direction[1]
        return (x >= 0) & (x < grid_rows) & (y >= 0) & (y < grid_cols)

    here = {direction: present(direction) for direction in AROUND}

    barrier = pltpu.get_barrier_semaphore()
    for direction in AROUND:

        @pl.when(here[direction])
        def _(direction=direction):
            pl.semaphore_signal(
                barrier,
                inc=1,
                device_id=(gx + direction[0], gy + direction[1]),
                device_id_type=MESH,
            )

    loads = [
        pltpu.make_async_copy(source, target, local_sem.at[n])
        for n, (source, target) in enumerate(
            [
                (u_hbm, u_ref),
                (v_hbm, v_ref),
                (mat_hbm, mat_ref),
                (intact_hbm, intact_ref),
                (bulk_hbm, bulk_ref),
                (shear_hbm, shear_ref),
                (dens_hbm, dens_ref),
            ]
        )
    ]
    for load in loads:
        load.start()

    def side(value):
        return 0 if value < 0 else 1

    def slab(name, key):
        if name == "u":
            return u_slab
        if name == "m":
            return m_slab
        if name == "v":
            return v_slab
        buf = t_slab if name[0] == "t" else f_slab
        return buf.at[name[1], side(-key[1][0])]

    def ends(name, key, whole):
        number = number_of[name]
        if key[1][1] == 0:
            first = rows if key[0] == "C" else 0
            return whole.at[:, first : first + REACH], slab(name, key)
        at, size, _ = place[number, key]
        return send_buf.at[at : at + size], recv_buf.at[at : at + size]

    def copy_to(name, key, whole):
        dx, dy = key[1]
        source, target = ends(name, key, whole)
        return pltpu.make_async_remote_copy(
            src_ref=source,
            dst_ref=target,
            send_sem=send_sem.at[number_of[name], SLOT[key]],
            recv_sem=recv_sem.at[number_of[name], SLOT[key]],
            device_id=(gx + dx, gy + dy),
            device_id_type=MESH,
        )

    def pack(name, keys, whole, first_col):
        number = number_of[name]
        comps = listed[number][2]
        for key in keys:
            if key[1][1] == 0:
                continue
            at, _, runs = place[number, key]
            for comp in range(comps):
                for row, col, width in runs:
                    begin = first_col + col
                    send_buf[at : at + width] = whole[comp, row, begin : begin + width]
                    at += width

    def start_all(name, keys, whole):
        for key in keys:

            @pl.when(here[key[1]])
            def _(key=key):
                copy_to(name, key, whole).start()

    def wait_recv(name, key, whole):
        _, target = ends(name, key, whole)
        pltpu.make_async_remote_copy(
            src_ref=target,
            dst_ref=target,
            send_sem=send_sem.at[number_of[name], SLOT[key]],
            recv_sem=recv_sem.at[number_of[name], SLOT[key]],
            device_id=(gx - key[1][0], gy - key[1][1]),
            device_id_type=MESH,
        ).wait_recv()

    def wait_sends(name, keys, whole):
        for key in keys:

            @pl.when(here[key[1]])
            def _(key=key):
                copy_to(name, key, whole).wait_send()

    def landed(name, key):
        number = number_of[name]
        at, _, runs = place[number, key]
        dx, dy = key[1]
        for comp in range(listed[number][2]):
            for row, col, width in runs:
                yield comp, row - dx * rows, REACH + col - dy * cols, at, width
                at += width

    def take_state(name, own, wide):
        for key in STATE:
            origin = (-key[1][0], -key[1][1])

            @pl.when(here[origin])
            def _(key=key, origin=origin):
                wait_recv(name, key, own)
                if origin[1] == 0:
                    buf = slab(name, key)
                    for comp in range(own.shape[0]):
                        for r in range(REACH):
                            wide[comp, rows + r, REACH : REACH + cols] = buf[comp, r]
                    return
                for comp, row, col, at, width in landed(name, key):
                    wide[comp, row, col : col + width] = recv_buf[at : at + width]

    def take_sums(name, keys, whole):
        comps = whole.shape[0]
        wait_sends(name, [key for key in keys if key[1][1] == 0], whole)
        for key in keys:
            origin = (-key[1][0], -key[1][1])

            @pl.when(here[origin])
            def _(key=key, origin=origin):
                wait_recv(name, key, whole)
                if origin[1] == 0:
                    buf = slab(name, key)
                    first = (rows if key[0] == "C" else 0) + origin[0] * rows
                    for comp in range(comps):
                        for n in range(REACH):
                            whole[comp, first + n] = whole[comp, first + n] + buf[comp, n]
                    return
                for comp, row, col, at, width in landed(name, key):
                    span = slice(col, col + width)
                    whole[comp, row, span] = whole[comp, row, span] + recv_buf[at : at + width]

    loads[0].wait()
    pack("u", STATE, u_ref, 0)

    on_x = (gx > 0).astype(jnp.int32) + (gx < grid_rows - 1).astype(jnp.int32)
    on_y = (gy > 0).astype(jnp.int32) + (gy < grid_cols - 1).astype(jnp.int32)
    pl.semaphore_wait(barrier, (1 + on_x) * (1 + on_y) - 1)
    start_all("u", STATE, u_ref)

    loads[1].wait()
    loads[2].wait()
    mat_f32[0] = mat_ref[...].astype(F32)
    pack("m", STATE, mat_f32, 0)
    pack("v", STATE, v_ref, 0)

    wide_u[...] = jnp.zeros(wide_u.shape, F32)
    wide_v[...] = jnp.zeros(wide_v.shape, F32)
    wide_m[...] = jnp.zeros(wide_m.shape, F32)
    for comp in range(3):
        wide_u[comp, 0:rows, REACH : REACH + cols] = u_ref[comp]
        wide_v[comp, 0:rows, REACH : REACH + cols] = v_ref[comp]
    wide_m[0, 0:rows, REACH : REACH + cols] = mat_f32[0]

    def shifted(values, c):
        if c == 0:
            return values
        lane = lax.broadcasted_iota(jnp.int32, values.shape, 1)
        moved = pltpu.roll(values, (-c) % nz, axis=1)
        return jnp.where((lane + c >= 0) & (lane + c < nz), moved, 0.0)

    def shift_motion():
        for r in range(wide_rows):
            for comp in range(3):
                values = wide_u[comp, r]
                for c in range(-NEAR, NEAR + 1):
                    moved = shifted(values, c)
                    if comp == 2 and c != 0:
                        moved = moved + float(c)
                    u_shift[c + NEAR, comp, r] = moved

    def materials():
        for r in range(wide_rows):
            classes = wide_m[0, r]
            bulk = jnp.full(classes.shape, bulk_ref[0], F32)
            shear = jnp.full(classes.shape, shear_ref[0], F32)
            dens = jnp.full(classes.shape, dens_ref[0], F32)
            for number in range(1, bulk_ref.shape[0]):
                match = classes == float(number)
                bulk = jnp.where(match, bulk_ref[number], bulk)
                shear = jnp.where(match, shear_ref[number], shear)
                dens = jnp.where(match, dens_ref[number], dens)
            inertia[r] = TIME_STEP / dens
            a_coef[r] = (9.0 / (VOLUME * VOLUME)) * (bulk - (5.0 / 3.0) * shear)
            stiff = (15.0 / VOLUME) * shear
            for c in range(-NEAR, NEAR + 1):
                b_shift[c + NEAR, r] = shifted(stiff, c)

    depth = lax.broadcasted_iota(jnp.int32, (cols, nz), 1)
    column = lax.broadcasted_iota(jnp.int32, (cols, nz), 0) + gy * cols

    def partner(buffer, i, a, b, c, own):
        if c > NEAR:
            return shifted(own, c)
        return buffer[c + NEAR, i + a, pl.ds(REACH + b, cols)]

    def bond_vector(i, a, b, c, own):
        y = []
        for comp in range(3):
            if c > NEAR:
                there = shifted(own[3][comp], c)
                if comp == 2:
                    there = there + float(c)
            else:
                there = u_shift[c + NEAR, comp, i + a, pl.ds(REACH + b, cols)]
            y.append(there - (own[0][a], own[1][b], own[2])[comp])
        return y

    def geometry(i, a, b, c, own):
        y0, y1, y2 = bond_vector(i, a, b, c, own)
        square = y0 * y0 + y1 * y1 + y2 * y2
        inverse = lax.rsqrt(square)
        return square * inverse, inverse

    def own_motion(i):
        mine = [wide_u[comp, i, REACH : REACH + cols] for comp in range(3)]
        by_row = {a: mine[0] - float(a) for a in range(REACH + 1)}
        by_col = {b: mine[1] - float(b) for b in range(-REACH, REACH + 1)}
        return (by_row, by_col, mine[2], mine)

    def back(values, c):
        return values if c == 0 else pltpu.roll(values, c % nz, axis=1)

    def order(t):
        return lax.rem(t + rows - REACH, rows)

    def send_done(t, name, keys, whole):
        @pl.when(t == REACH - 1)
        def _():
            pack(name, keys["C"], whole, REACH)
            start_all(name, keys["C"], whole)

        @pl.when(t == 2 * REACH - 1)
        def _():
            pack(name, keys["A"], whole, REACH)
            start_all(name, keys["A"], whole)

    def weights():
        @pl.loop(0, rows)
        def _(i):
            lane_in = {
                c: jnp.where((depth + c >= 0) & (depth + c < nz), 1.0, 0.0)
                for c in range(-NEAR, REACH + 1)
            }
            for (a, b), members in GROUPS.items():
                row_in = (gx * rows + i + a) < grid_rows * rows
                plane = jnp.where(
                    (column + b >= 0) & (column + b < grid_cols * cols) & row_in, 1.0, 0.0
                )
                for k, c in members:
                    flag[k, i] = intact_ref[k, i].astype(F32) * (plane * lane_in[c])

    def prepare():
        @pl.loop(0, rows)
        def _(i):
            own_b = b_shift[NEAR, i, pl.ds(REACH, cols)]
            for k, (a, b, c) in enumerate(OFFSETS):
                both_b = own_b + partner(b_shift, i, a, b, c, own_b)
                scale = flag[k, i] * by_inverse[k, i]
                by_stretch[k, i] = scale * (both_b * (by_stretch[k, i] * (1.0 / RADII[k])))
                by_inverse[k, i] = scale

    def strain_pass(send):
        strain[...] = jnp.zeros(strain.shape, F32)

        @pl.loop(0, rows)
        def _(t):
            i = order(t)
            own = own_motion(i)
            sums = []
            for (a, b), members in GROUPS.items():
                returned = []
                for k, c in members:
                    length, inverse = geometry(i, a, b, c, own)
                    stretch = length - RADII[k]
                    by_inverse[k, i] = inverse
                    by_stretch[k, i] = stretch
                    term = flag[k, i] * stretch
                    sums.append(term)
                    returned.append(back(term, c))
                at = pl.ds(REACH + b, cols)
                strain[0, i + a, at] = strain[0, i + a, at] + tree_sum(returned)
                sums = [tree_sum(sums)]
            at = pl.ds(REACH, cols)
            strain[0, i, at] = strain[0, i, at] + sums[0]
            send(t)

    def force_pass(send):
        force[...] = jnp.zeros(force.shape, F32)

        @pl.loop(0, rows)
        def _(t):
            i = order(t)
            own = own_motion(i)
            mid = pl.ds(REACH, cols)
            own_a = a_shift[NEAR, i, mid]
            sums = [[], [], []]
            for (a, b), members in GROUPS.items():
                at = pl.ds(REACH + b, cols)
                returned = [[], [], []]
                for k, c in members:
                    y = bond_vector(i, a, b, c, own)
                    both_a = own_a + partner(a_shift, i, a, b, c, own_a)
                    tension = by_inverse[k, i] * both_a + by_stretch[k, i]
                    for comp in range(3):
                        term = tension * y[comp]
                        sums[comp].append(term)
                        returned[comp].append(back(term, c))
                for comp in range(3):
                    force[comp, i + a, at] = force[comp, i + a, at] - tree_sum(returned[comp])
                    sums[comp] = [tree_sum(sums[comp])]
            for comp in range(3):
                force[comp, i, mid] = force[comp, i, mid] + sums[comp][0]

            send(t)

    for load in loads[3:]:
        load.wait()
    weights()
    take_state("u", u_ref, wide_u)
    start_all("m", STATE, mat_f32)
    shift_motion()

    for step in range(STEPS):
        last = step == STEPS - 1
        name = ("t", step)
        every = keys_of("sum")
        strain_pass(lambda t, name=name: send_done(t, name, CHUNKS, strain))
        pack(name, CHUNKS["B"], strain, REACH)
        start_all(name, CHUNKS["B"], strain)
        if step == 0:
            start_all("v", STATE, v_ref)
            take_state("m", mat_f32, wide_m)
            materials()
        prepare()
        take_sums(name, every, strain)

        for r in range(wide_rows):
            values = strain[0, r] * a_coef[r]
            for c in range(-NEAR, NEAR + 1):
                a_shift[c + NEAR, r] = shifted(values, c)

        wait_sends(name, [key for key in every if key[1][1] != 0], strain)
        name = ("f", step)
        keys = FINAL if last else CHUNKS
        every = keys_of("final" if last else "sum")
        force_pass(lambda t, name=name, keys=keys: send_done(t, name, keys, force))
        pack(name, keys["B"], force, REACH)
        start_all(name, keys["B"], force)
        if step == 0:
            take_state("v", v_ref, wide_v)
        take_sums(name, every, force)
        if not last:
            for r in range(wide_rows):
                for comp in range(3):
                    speed = wide_v[comp, r] + force[comp, r] * inertia[r]
                    wide_v[comp, r] = speed
                    wide_u[comp, r] = wide_u[comp, r] + TIME_STEP * speed

            shift_motion()
        else:
            mid = pl.ds(REACH, cols)
            for r in range(rows):
                for comp in range(3):
                    pull = force[comp, r, mid]
                    speed = wide_v[comp, r, mid] + pull * inertia[r, mid]
                    out_f[comp, r] = pull
                    out_v[comp, r] = speed
                    out_u[comp, r] = wide_u[comp, r, mid] + TIME_STEP * speed

        wait_sends(name, [key for key in every if key[1][1] != 0], force)
    for name, own in (("u", u_ref), ("m", mat_f32), ("v", v_ref)):
        wait_sends(name, STATE, own)


def hand_over(u_in, v_in, f_in, u_out, v_out, f_out):
    u_out[...] = u_in[...]
    v_out[...] = v_in[...]
    f_out[...] = f_in[...]


def on_device(displacement, velocity, intact, material, bulk_modulus, shear_modulus, density):
    rows, cols, nz = material.shape
    wide_rows = rows + REACH
    padded = round_up(cols + 2 * REACH, 8)
    packed = layout(rows, cols)[1]
    own = jax.ShapeDtypeStruct((3, rows, cols, nz), F32)
    vmem = pl.BlockSpec(memory_space=pltpu.VMEM)
    hbm = pl.BlockSpec(memory_space=pltpu.HBM)
    table = pltpu.SMEM(bulk_modulus.shape, F32)

    def buffer(*shape):
        return pltpu.VMEM(shape + (nz,), F32)

    results = pl.pallas_call(
        functools.partial(kernel, lax.axis_size("gx"), lax.axis_size("gy")),
        out_shape=(own, own, own),
        in_specs=[hbm] * 7,
        out_specs=(vmem, vmem, vmem),
        scratch_shapes=[
            buffer(3, rows, cols),
            buffer(3, rows, cols),
            pltpu.VMEM(material.shape, jnp.int32),
            buffer(1, rows, cols),
            table,
            table,
            table,
            pltpu.VMEM(intact.shape, jnp.int32),
            pltpu.VMEM(intact.shape, F32),
            pltpu.VMEM(intact.shape, F32),
            pltpu.VMEM(intact.shape, F32),
            buffer(3, wide_rows, padded),
            buffer(3, wide_rows, padded),
            buffer(1, wide_rows, padded),
            buffer(5, 3, wide_rows, padded),
            buffer(5, wide_rows, padded),
            buffer(5, wide_rows, padded),
            buffer(wide_rows, padded),
            buffer(wide_rows, padded),
            buffer(1, wide_rows, padded),
            buffer(3, wide_rows, padded),
            buffer(packed),
            buffer(packed),
            buffer(3, REACH, cols),
            buffer(1, REACH, cols),
            buffer(3, REACH, cols),
            buffer(STEPS, 2, 1, REACH, padded),
            buffer(STEPS, 2, 3, REACH, padded),
            pltpu.SemaphoreType.DMA((7,)),
            pltpu.SemaphoreType.DMA((len(stages()), 12)),
            pltpu.SemaphoreType.DMA((len(stages()), 12)),
        ],
        compiler_params=pltpu.CompilerParams(
            collective_id=0, has_side_effects=True, vmem_limit_bytes=67_043_328
        ),
        name="peridynamics",
    )(displacement, velocity, intact, material, bulk_modulus, shear_modulus, density)
    return pl.pallas_call(
        hand_over,
        out_shape=(own, own, own),
        in_specs=[vmem] * 3,
        out_specs=(vmem, vmem, vmem),
        name="hand_over",
    )(*results)


def solution(mesh):
    node = P(None, "gx", "gy", None)
    return jax.shard_map(
        on_device,
        mesh=mesh,
        in_specs=(node, node, node, P("gx", "gy", None), P(), P(), P()),
        out_specs=(node, node, node),
        check_vma=False,
    )
```

```python
import functools
import math

import jax
import jax.numpy as jnp
from jax import lax
from jax.experimental import pallas as pl
from jax.experimental.pallas import tpu as pltpu
from jax.sharding import PartitionSpec as P

STEPS = 2
TIME_STEP = 0.02
REACH = 3
NEAR = 2
MESH = pl.DeviceIdType.MESH
F32 = jnp.float32

AROUND = [(dx, dy) for dx in (-1, 0, 1) for dy in (-1, 0, 1) if (dx, dy) != (0, 0)]
STATE = [("S", (-1, 0)), ("S", (0, -1)), ("S", (0, 1)), ("S", (-1, -1)), ("S", (-1, 1))]
CHUNKS = {
    "C": [("C", (1, -1)), ("C", (1, 1)), ("C", (0, -1)), ("C", (0, 1)), ("C", (1, 0))],
    "A": [("A", (-1, -1)), ("A", (-1, 1)), ("A", (0, -1)), ("A", (0, 1)), ("A", (-1, 0))],
    "B": [("B", (0, -1)), ("B", (0, 1))],
}
FINAL = {
    "C": [("C", (1, -1)), ("C", (1, 1)), ("C", (1, 0))],
    "A": [("A", (0, -1)), ("A", (0, 1))],
    "B": [("B", (0, -1)), ("B", (0, 1))],
}
SLOT = {key: n for n, key in enumerate(CHUNKS["C"] + CHUNKS["A"] + CHUNKS["B"])}
SLOT.update({key: n for n, key in enumerate(STATE)})


def half_offsets():
    span = range(-REACH, REACH + 1)
    return [
        (a, b, c)
        for a in span
        for b in span
        for c in span
        if a * a + b * b + c * c <= REACH * REACH and (a, b, c) > (0, 0, 0)
    ]


OFFSETS = half_offsets()
GROUPS = {}
for _k, (_a, _b, _c) in enumerate(OFFSETS):
    GROUPS.setdefault((_a, _b), []).append((_k, _c))
RADII = [math.sqrt(float(a * a + b * b + c * c)) for a, b, c in OFFSETS]
VOLUME = 2.0 * sum(RADII)


def round_up(value, unit):
    return -(-value // unit) * unit


AT_PARTNER = [(1, -1), (1, 1), (2, -1), (2, 1)]


def bond_order(rows):
    tail = range(rows - REACH, rows)
    groups = list(GROUPS)
    return [
        ("C", [(i, [(a, b) for a, b in groups if i + a >= rows]) for i in tail]),
        ("A", [(i, groups) for i in range(REACH)]),
        (
            "B",
            [(i, groups) for i in range(REACH, rows - REACH)]
            + [(i, [(a, b) for a, b in groups if i + a < rows]) for i in tail],
        ),
    ]


def spans(rows, cols, key, kind):
    chunk, (dx, dy) = key
    own = {(r, c) for r in range(rows) for c in range(cols)}
    wide = own | {(r + a, c + b) for r, c in own for a, b in GROUPS}
    sender = own if kind == "state" else wide
    receiver = own if kind == "final" else wide
    first, end = {
        "A": (0, REACH), "B": (REACH, rows), "C": (rows, rows + REACH), "S": (0, rows)
    }[chunk]
    runs = []
    for row in range(first, end):
        used = [c for r, c in sender if r == row and (r - dx * rows, c - dy * cols) in receiver]
        if used:
            runs.append((row, min(used), max(used) + 1 - min(used)))
    return runs


def stages():
    listed = [("u", "state", 3), ("m", "state", 1), ("v", "state", 3)]
    for step in range(STEPS):
        listed.append((("t", step), "sum", 1))
        listed.append((("f", step), "final" if step == STEPS - 1 else "sum", 3))
    return listed


def keys_of(kind):
    if kind == "state":
        return STATE
    chunks = FINAL if kind == "final" else CHUNKS
    return chunks["C"] + chunks["A"] + chunks["B"]


def layout(rows, cols):
    place, at = {}, 0
    for number, (_, kind, comps) in enumerate(stages()):
        for key in keys_of(kind):
            if key[1][1] == 0:
                continue
            runs = spans(rows, cols, key, kind)
            size = round_up(comps * sum(width for _, _, width in runs), 8)
            place[number, key] = (at, size, runs)
            at += size
    return place, at


def tree_sum(terms):
    while len(terms) > 1:
        terms = [
            terms[n] + terms[n + 1] if n + 1 < len(terms) else terms[n]
            for n in range(0, len(terms), 2)
        ]
    return terms[0]


def kernel(
    grid_rows,
    grid_cols,
    u_hbm,
    v_hbm,
    intact_hbm,
    mat_hbm,
    bulk_hbm,
    shear_hbm,
    dens_hbm,
    out_u,
    out_v,
    out_f,
    u_ref,
    v_ref,
    mat_ref,
    mat_f32,
    bulk_ref,
    shear_ref,
    dens_ref,
    intact_ref,
    flag,
    by_inverse,
    by_stretch,
    wide_u,
    wide_v,
    wide_m,
    u_shift,
    a_shift,
    b_shift,
    a_coef,
    inertia,
    strain,
    force,
    send_buf,
    recv_buf,
    u_slab,
    m_slab,
    v_slab,
    t_slab,
    f_slab,
    local_sem,
    send_sem,
    recv_sem,
):
    rows, cols, nz = mat_ref.shape
    wide_rows = rows + REACH
    gx = lax.axis_index("gx")
    gy = lax.axis_index("gy")
    place, _ = layout(rows, cols)
    listed = stages()
    number_of = {name: number for number, (name, _, _) in enumerate(listed)}

    def present(direction):
        x = gx + direction[0]
        y = gy + direction[1]
        return (x >= 0) & (x < grid_rows) & (y >= 0) & (y < grid_cols)

    here = {direction: present(direction) for direction in AROUND}

    barrier = pltpu.get_barrier_semaphore()
    for direction in AROUND:

        @pl.when(here[direction])
        def _(direction=direction):
            pl.semaphore_signal(
                barrier,
                inc=1,
                device_id=(gx + direction[0], gy + direction[1]),
                device_id_type=MESH,
            )

    loads = [
        pltpu.make_async_copy(source, target, local_sem.at[n])
        for n, (source, target) in enumerate(
            [
                (u_hbm, u_ref),
                (v_hbm, v_ref),
                (mat_hbm, mat_ref),
                (intact_hbm, intact_ref),
                (bulk_hbm, bulk_ref),
                (shear_hbm, shear_ref),
                (dens_hbm, dens_ref),
            ]
        )
    ]
    for load in loads:
        load.start()

    def side(value):
        return 0 if value < 0 else 1

    def slab(name, key):
        if name == "u":
            return u_slab
        if name == "m":
            return m_slab
        if name == "v":
            return v_slab
        buf = t_slab if name[0] == "t" else f_slab
        return buf.at[name[1], side(-key[1][0])]

    def ends(name, key, whole):
        number = number_of[name]
        if key[1][1] == 0:
            first = rows if key[0] == "C" else 0
            return whole.at[:, first : first + REACH], slab(name, key)
        at, size, _ = place[number, key]
        return send_buf.at[at : at + size], recv_buf.at[at : at + size]

    def copy_to(name, key, whole):
        dx, dy = key[1]
        source, target = ends(name, key, whole)
        return pltpu.make_async_remote_copy(
            src_ref=source,
            dst_ref=target,
            send_sem=send_sem.at[number_of[name], SLOT[key]],
            recv_sem=recv_sem.at[number_of[name], SLOT[key]],
            device_id=(gx + dx, gy + dy),
            device_id_type=MESH,
        )

    def pack(name, keys, whole, first_col):
        number = number_of[name]
        comps = listed[number][2]
        for key in keys:
            if key[1][1] == 0:
                continue
            at, _, runs = place[number, key]
            for comp in range(comps):
                for row, col, width in runs:
                    begin = first_col + col
                    send_buf[at : at + width] = whole[comp, row, begin : begin + width]
                    at += width

    def start_all(name, keys, whole):
        for key in keys:

            @pl.when(here[key[1]])
            def _(key=key):
                copy_to(name, key, whole).start()

    def wait_recv(name, key, whole):
        _, target = ends(name, key, whole)
        pltpu.make_async_remote_copy(
            src_ref=target,
            dst_ref=target,
            send_sem=send_sem.at[number_of[name], SLOT[key]],
            recv_sem=recv_sem.at[number_of[name], SLOT[key]],
            device_id=(gx - key[1][0], gy - key[1][1]),
            device_id_type=MESH,
        ).wait_recv()

    def wait_sends(name, keys, whole):
        for key in keys:

            @pl.when(here[key[1]])
            def _(key=key):
                copy_to(name, key, whole).wait_send()

    def landed(name, key):
        number = number_of[name]
        at, _, runs = place[number, key]
        dx, dy = key[1]
        for comp in range(listed[number][2]):
            for row, col, width in runs:
                yield comp, row - dx * rows, REACH + col - dy * cols, at, width
                at += width

    def take_state(name, own, wide):
        for key in STATE:
            origin = (-key[1][0], -key[1][1])

            @pl.when(here[origin])
            def _(key=key, origin=origin):
                wait_recv(name, key, own)
                if origin[1] == 0:
                    buf = slab(name, key)
                    for comp in range(own.shape[0]):
                        for r in range(REACH):
                            wide[comp, rows + r, REACH : REACH + cols] = buf[comp, r]
                    return
                for comp, row, col, at, width in landed(name, key):
                    wide[comp, row, col : col + width] = recv_buf[at : at + width]

    def take_sums(name, keys, whole):
        comps = whole.shape[0]
        wait_sends(name, [key for key in keys if key[1][1] == 0], whole)
        for key in keys:
            origin = (-key[1][0], -key[1][1])

            @pl.when(here[origin])
            def _(key=key, origin=origin):
                wait_recv(name, key, whole)
                if origin[1] == 0:
                    buf = slab(name, key)
                    first = (rows if key[0] == "C" else 0) + origin[0] * rows
                    for comp in range(comps):
                        for n in range(REACH):
                            whole[comp, first + n] = whole[comp, first + n] + buf[comp, n]
                    return
                for comp, row, col, at, width in landed(name, key):
                    span = slice(col, col + width)
                    whole[comp, row, span] = whole[comp, row, span] + recv_buf[at : at + width]

    loads[0].wait()
    pack("u", STATE, u_ref, 0)

    on_x = (gx > 0).astype(jnp.int32) + (gx < grid_rows - 1).astype(jnp.int32)
    on_y = (gy > 0).astype(jnp.int32) + (gy < grid_cols - 1).astype(jnp.int32)
    pl.semaphore_wait(barrier, (1 + on_x) * (1 + on_y) - 1)
    start_all("u", STATE, u_ref)

    loads[1].wait()
    loads[2].wait()
    mat_f32[0] = mat_ref[...].astype(F32)
    pack("m", STATE, mat_f32, 0)
    pack("v", STATE, v_ref, 0)

    wide_u[...] = jnp.zeros(wide_u.shape, F32)
    wide_v[...] = jnp.zeros(wide_v.shape, F32)
    wide_m[...] = jnp.zeros(wide_m.shape, F32)
    for comp in range(3):
        wide_u[comp, 0:rows, REACH : REACH + cols] = u_ref[comp]
        wide_v[comp, 0:rows, REACH : REACH + cols] = v_ref[comp]
    wide_m[0, 0:rows, REACH : REACH + cols] = mat_f32[0]

    def shifted(values, c):
        if c == 0:
            return values
        lane = lax.broadcasted_iota(jnp.int32, values.shape, 1)
        moved = pltpu.roll(values, (-c) % nz, axis=1)
        return jnp.where((lane + c >= 0) & (lane + c < nz), moved, 0.0)

    def shift_motion():
        for r in range(wide_rows):
            for comp in range(3):
                values = wide_u[comp, r]
                for c in range(-NEAR, NEAR + 1):
                    moved = shifted(values, c)
                    if comp == 2 and c != 0:
                        moved = moved + float(c)
                    u_shift[c + NEAR, comp, r] = moved

    def materials():
        for r in range(wide_rows):
            classes = wide_m[0, r]
            bulk = jnp.full(classes.shape, bulk_ref[0], F32)
            shear = jnp.full(classes.shape, shear_ref[0], F32)
            dens = jnp.full(classes.shape, dens_ref[0], F32)
            for number in range(1, bulk_ref.shape[0]):
                match = classes == float(number)
                bulk = jnp.where(match, bulk_ref[number], bulk)
                shear = jnp.where(match, shear_ref[number], shear)
                dens = jnp.where(match, dens_ref[number], dens)
            inertia[r] = TIME_STEP / dens
            a_coef[r] = (9.0 / (VOLUME * VOLUME)) * (bulk - (5.0 / 3.0) * shear)
            stiff = (15.0 / VOLUME) * shear
            for c in range(-NEAR, NEAR + 1):
                b_shift[c + NEAR, r] = shifted(stiff, c)

    depth = lax.broadcasted_iota(jnp.int32, (cols, nz), 1)
    column = lax.broadcasted_iota(jnp.int32, (cols, nz), 0) + gy * cols

    def partner(buffer, i, a, b, c, own):
        if c > NEAR:
            return shifted(own, c)
        return buffer[c + NEAR, i + a, pl.ds(REACH + b, cols)]

    def bond_vector(i, a, b, c, own):
        y = []
        for comp in range(3):
            if c > NEAR:
                there = shifted(own[3][comp], c)
                if comp == 2:
                    there = there + float(c)
            else:
                there = u_shift[c + NEAR, comp, i + a, pl.ds(REACH + b, cols)]
            y.append(there - (own[0][a], own[1][b], own[2])[comp])
        return y

    def geometry(i, a, b, c, own):
        y0, y1, y2 = bond_vector(i, a, b, c, own)
        square = y0 * y0 + y1 * y1 + y2 * y2
        inverse = lax.rsqrt(square)
        return square * inverse, inverse

    def own_motion(i):
        mine = [wide_u[comp, i, REACH : REACH + cols] for comp in range(3)]
        by_row = {a: mine[0] - float(a) for a in range(REACH + 1)}
        by_col = {b: mine[1] - float(b) for b in range(-REACH, REACH + 1)}
        return (by_row, by_col, mine[2], mine)

    def back(values, c):
        return values if c == 0 else pltpu.roll(values, c % nz, axis=1)

    def send_done(name, chunk, keys, whole):
        pack(name, keys[chunk], whole, REACH)
        start_all(name, keys[chunk], whole)

    def weights():
        @pl.loop(0, rows)
        def _(i):
            lane_in = {
                c: jnp.where((depth + c >= 0) & (depth + c < nz), 1.0, 0.0)
                for c in range(-NEAR, REACH + 1)
            }
            for (a, b), members in GROUPS.items():
                row_in = (gx * rows + i + a) < grid_rows * rows
                plane = jnp.where(
                    (column + b >= 0) & (column + b < grid_cols * cols) & row_in, 1.0, 0.0
                )
                for k, c in members:
                    flag[k, i] = intact_ref[k, i].astype(F32) * (plane * lane_in[c])

    def prepare():
        @pl.loop(0, rows)
        def _(i):
            own_b = b_shift[NEAR, i, pl.ds(REACH, cols)]
            for k, (a, b, c) in enumerate(OFFSETS):
                both_b = own_b + partner(b_shift, i, a, b, c, own_b)
                scale = flag[k, i] * by_inverse[k, i]
                by_stretch[k, i] = scale * (both_b * (by_stretch[k, i] * (1.0 / RADII[k])))
                by_inverse[k, i] = scale

    def strain_pass(send):
        strain[...] = jnp.zeros(strain.shape, F32)
        mid = pl.ds(REACH, cols)
        for chunk, work in bond_order(rows):
            for i, groups in work:
                own = own_motion(i)
                sums = []
                for a, b in groups:
                    returned = []
                    for k, c in GROUPS[a, b]:
                        length, inverse = geometry(i, a, b, c, own)
                        stretch = length - RADII[k]
                        by_inverse[k, i] = inverse
                        by_stretch[k, i] = stretch
                        term = flag[k, i] * stretch
                        sums.append(term)
                        returned.append(back(term, c))
                    at = pl.ds(REACH + b, cols)
                    strain[0, i + a, at] = strain[0, i + a, at] + tree_sum(returned)
                    sums = [tree_sum(sums)]
                strain[0, i, mid] = strain[0, i, mid] + sums[0]
            send(chunk)

    def force_pass(send):
        force[...] = jnp.zeros(force.shape, F32)
        mid = pl.ds(REACH, cols)
        for chunk, work in bond_order(rows):
            for i, groups in work:
                own = own_motion(i)
                own_a = a_shift[NEAR, i, mid]
                sums = [[], [], []]
                for a, b in groups:
                    at = pl.ds(REACH + b, cols)
                    tensions = []
                    for k, c in GROUPS[a, b]:
                        both_a = own_a + partner(a_shift, i, a, b, c, own_a)
                        tensions.append((c, by_inverse[k, i] * both_a + by_stretch[k, i]))
                    if (a, b) in AT_PARTNER:
                        base = (own[0][a], own[1][b], own[2])
                        shift = (float(a), float(b), 0.0)
                        pulled = [(c, back(tension, c)) for c, tension in tensions]
                        here_all = tree_sum([tension for _, tension in tensions])
                        there_all = tree_sum([tension for _, tension in pulled])
                        for comp in range(3):
                            direct = tree_sum(
                                [t * u_shift[c + NEAR, comp, i + a, at] for c, t in tensions]
                            )
                            sums[comp].append(direct - base[comp] * here_all)
                            origin = tree_sum(
                                [t * u_shift[NEAR - c, comp, i, mid] for c, t in pulled]
                            )
                            end = u_shift[NEAR, comp, i + a, at] + shift[comp]
                            force[comp, i + a, at] = force[comp, i + a, at] + (
                                origin - end * there_all
                            )
                    else:
                        returned = [[], [], []]
                        for c, tension in tensions:
                            y = bond_vector(i, a, b, c, own)
                            for comp in range(3):
                                term = tension * y[comp]
                                sums[comp].append(term)
                                returned[comp].append(back(term, c))
                        for comp in range(3):
                            force[comp, i + a, at] = force[comp, i + a, at] - tree_sum(
                                returned[comp]
                            )
                    sums = [[tree_sum(sums[comp])] for comp in range(3)]
                for comp in range(3):
                    force[comp, i, mid] = force[comp, i, mid] + sums[comp][0]
            send(chunk)

    for load in loads[3:]:
        load.wait()
    weights()
    take_state("u", u_ref, wide_u)
    start_all("m", STATE, mat_f32)
    shift_motion()

    for step in range(STEPS):
        last = step == STEPS - 1
        name = ("t", step)
        every = keys_of("sum")
        strain_pass(lambda chunk, name=name: send_done(name, chunk, CHUNKS, strain))
        if step == 0:
            start_all("v", STATE, v_ref)
            take_state("m", mat_f32, wide_m)
            materials()
        prepare()
        take_sums(name, every, strain)

        for r in range(wide_rows):
            values = strain[0, r] * a_coef[r]
            for c in range(-NEAR, NEAR + 1):
                a_shift[c + NEAR, r] = shifted(values, c)

        wait_sends(name, [key for key in every if key[1][1] != 0], strain)
        name = ("f", step)
        keys = FINAL if last else CHUNKS
        every = keys_of("final" if last else "sum")
        force_pass(lambda chunk, name=name, keys=keys: send_done(name, chunk, keys, force))
        if step == 0:
            take_state("v", v_ref, wide_v)
        take_sums(name, every, force)
        if not last:
            for r in range(wide_rows):
                for comp in range(3):
                    speed = wide_v[comp, r] + force[comp, r] * inertia[r]
                    wide_v[comp, r] = speed
                    wide_u[comp, r] = wide_u[comp, r] + TIME_STEP * speed

            shift_motion()
        else:
            mid = pl.ds(REACH, cols)
            for r in range(rows):
                for comp in range(3):
                    pull = force[comp, r, mid]
                    speed = wide_v[comp, r, mid] + pull * inertia[r, mid]
                    out_f[comp, r] = pull
                    out_v[comp, r] = speed
                    out_u[comp, r] = wide_u[comp, r, mid] + TIME_STEP * speed

        wait_sends(name, [key for key in every if key[1][1] != 0], force)
    for name, own in (("u", u_ref), ("m", mat_f32), ("v", v_ref)):
        wait_sends(name, STATE, own)


def hand_over(u_in, v_in, f_in, u_out, v_out, f_out):
    u_out[...] = u_in[...]
    v_out[...] = v_in[...]
    f_out[...] = f_in[...]


def on_device(displacement, velocity, intact, material, bulk_modulus, shear_modulus, density):
    rows, cols, nz = material.shape
    wide_rows = rows + REACH
    padded = round_up(cols + 2 * REACH, 8)
    packed = layout(rows, cols)[1]
    own = jax.ShapeDtypeStruct((3, rows, cols, nz), F32)
    vmem = pl.BlockSpec(memory_space=pltpu.VMEM)
    hbm = pl.BlockSpec(memory_space=pltpu.HBM)
    table = pltpu.SMEM(bulk_modulus.shape, F32)

    def buffer(*shape):
        return pltpu.VMEM(shape + (nz,), F32)

    results = pl.pallas_call(
        functools.partial(kernel, lax.axis_size("gx"), lax.axis_size("gy")),
        out_shape=(own, own, own),
        in_specs=[hbm] * 7,
        out_specs=(vmem, vmem, vmem),
        scratch_shapes=[
            buffer(3, rows, cols),
            buffer(3, rows, cols),
            pltpu.VMEM(material.shape, jnp.int32),
            buffer(1, rows, cols),
            table,
            table,
            table,
            pltpu.VMEM(intact.shape, jnp.int32),
            pltpu.VMEM(intact.shape, F32),
            pltpu.VMEM(intact.shape, F32),
            pltpu.VMEM(intact.shape, F32),
            buffer(3, wide_rows, padded),
            buffer(3, wide_rows, padded),
            buffer(1, wide_rows, padded),
            buffer(5, 3, wide_rows, padded),
            buffer(5, wide_rows, padded),
            buffer(5, wide_rows, padded),
            buffer(wide_rows, padded),
            buffer(wide_rows, padded),
            buffer(1, wide_rows, padded),
            buffer(3, wide_rows, padded),
            buffer(packed),
            buffer(packed),
            buffer(3, REACH, cols),
            buffer(1, REACH, cols),
            buffer(3, REACH, cols),
            buffer(STEPS, 2, 1, REACH, padded),
            buffer(STEPS, 2, 3, REACH, padded),
            pltpu.SemaphoreType.DMA((7,)),
            pltpu.SemaphoreType.DMA((len(stages()), 12)),
            pltpu.SemaphoreType.DMA((len(stages()), 12)),
        ],
        compiler_params=pltpu.CompilerParams(
            collective_id=0, has_side_effects=True, vmem_limit_bytes=67_043_328
        ),
        name="peridynamics",
    )(displacement, velocity, intact, material, bulk_modulus, shear_modulus, density)
    return pl.pallas_call(
        hand_over,
        out_shape=(own, own, own),
        in_specs=[vmem] * 3,
        out_specs=(vmem, vmem, vmem),
        name="hand_over",
    )(*results)


def solution(mesh):
    node = P(None, "gx", "gy", None)
    return jax.shard_map(
        on_device,
        mesh=mesh,
        in_specs=(node, node, node, P("gx", "gy", None), P(), P(), P()),
        out_specs=(node, node, node),
        check_vma=False,
    )
```

```python
import functools
import math

import jax
import jax.numpy as jnp
from jax import lax
from jax.experimental import pallas as pl
from jax.experimental.pallas import tpu as pltpu
from jax.sharding import PartitionSpec as P

STEPS = 2
TIME_STEP = 0.02
REACH = 3
NEAR = 2
MESH = pl.DeviceIdType.MESH
F32 = jnp.float32

AROUND = [(dx, dy) for dx in (-1, 0, 1) for dy in (-1, 0, 1) if (dx, dy) != (0, 0)]
STATE = [("S", (-1, 0)), ("S", (0, -1)), ("S", (0, 1)), ("S", (-1, -1)), ("S", (-1, 1))]
CHUNKS = {
    "C": [("C", (1, -1)), ("C", (1, 1)), ("C", (0, -1)), ("C", (0, 1)), ("C", (1, 0))],
    "A": [("A", (-1, -1)), ("A", (-1, 1)), ("A", (0, -1)), ("A", (0, 1)), ("A", (-1, 0))],
    "B": [("B", (0, -1)), ("B", (0, 1))],
    "E": [("E", (0, -1)), ("E", (0, 1))],
}
FINAL = {
    "C": [("C", (1, -1)), ("C", (1, 1)), ("C", (1, 0))],
    "A": [("A", (0, -1)), ("A", (0, 1))],
    "B": [("B", (0, -1)), ("B", (0, 1))],
    "E": [("E", (0, -1)), ("E", (0, 1))],
}
CROSSED = {
    "C": [("C", (1, 0))],
    "A": [("A", (-1, 0))],
    "B": [("B", (0, -1)), ("B", (0, 1))],
    "E": [("E", (0, -1)), ("E", (0, 1))],
    "A late": [("A", (0, -1)), ("A", (0, 1))],
    "C late": [("C", (0, -1)), ("C", (0, 1))],
}
ORDERS = {"sum": CHUNKS, "final": FINAL, "crossed": CROSSED}
SLOT = {key: n for n, key in enumerate(sum(CHUNKS.values(), []))}
SLOTS = len(SLOT)
SLOT.update({key: n for n, key in enumerate(STATE)})


def half_offsets():
    span = range(-REACH, REACH + 1)
    return [
        (a, b, c)
        for a in span
        for b in span
        for c in span
        if a * a + b * b + c * c <= REACH * REACH and (a, b, c) > (0, 0, 0)
    ]


OFFSETS = half_offsets()
GROUPS = {}
for _k, (_a, _b, _c) in enumerate(OFFSETS):
    GROUPS.setdefault((_a, _b), []).append((_k, _c))
RADII = [math.sqrt(float(a * a + b * b + c * c)) for a, b, c in OFFSETS]
VOLUME = 2.0 * sum(RADII)


def round_up(value, unit):
    return -(-value // unit) * unit


AT_PARTNER = [(a, b) for a in (1, 2) for b in (-2, -1, 1, 2)]


def bond_order(rows, order):
    tail = range(rows - REACH, rows)
    groups = list(GROUPS)
    work = {
        "C": [(i, [(a, b) for a, b in groups if i + a >= rows]) for i in tail],
        "A": [(i, groups) for i in range(REACH)],
        "B": [(i, groups) for i in range(REACH, rows - REACH)],
        "E": [(i, [(a, b) for a, b in groups if i + a < rows]) for i in tail],
    }
    return [(chunk, work[chunk]) for chunk in order]


def spans(rows, cols, key, kind):
    chunk, (dx, dy) = key
    own = {(r, c) for r in range(rows) for c in range(cols)}
    wide = own | {(r + a, c + b) for r, c in own for a, b in GROUPS}
    sender = own if kind == "state" else wide
    if kind == "crossed":
        sender = {(r + x, c) for r, c in wide for x in (-rows, 0, rows)}
    receiver = own if kind == "final" else wide
    first, end = {
        "A": (0, REACH),
        "B": (REACH, rows - REACH),
        "E": (rows - REACH, rows),
        "C": (rows, rows + REACH),
        "S": (0, rows),
    }[chunk]
    runs = []
    for row in range(first, end):
        used = [c for r, c in sender if r == row and (r - dx * rows, c - dy * cols) in receiver]
        if used:
            runs.append((row, min(used), max(used) + 1 - min(used)))
    return runs


def stages():
    listed = [("u", "state", 3), ("m", "state", 1), ("v", "state", 3)]
    for step in range(STEPS):
        listed.append((("t", step), "sum", 1))
        listed.append((("f", step), "final" if step == STEPS - 1 else "crossed", 3))
    return listed


def keys_of(kind):
    if kind == "state":
        return STATE
    return sum(ORDERS[kind].values(), [])


def layout(rows, cols):
    place, at = {}, 0
    for number, (_, kind, comps) in enumerate(stages()):
        for key in keys_of(kind):
            if key[1][1] == 0:
                continue
            runs = spans(rows, cols, key, kind)
            size = round_up(comps * sum(width for _, _, width in runs), 8)
            place[number, key] = (at, size, runs)
            at += size
    return place, at


def tree_sum(terms):
    while len(terms) > 1:
        terms = [
            terms[n] + terms[n + 1] if n + 1 < len(terms) else terms[n]
            for n in range(0, len(terms), 2)
        ]
    return terms[0]


def kernel(
    grid_rows,
    grid_cols,
    u_hbm,
    v_hbm,
    intact_hbm,
    mat_hbm,
    bulk_hbm,
    shear_hbm,
    dens_hbm,
    out_u,
    out_v,
    out_f,
    u_ref,
    v_ref,
    mat_ref,
    mat_f32,
    bulk_ref,
    shear_ref,
    dens_ref,
    intact_ref,
    flag,
    by_inverse,
    by_stretch,
    wide_u,
    wide_v,
    wide_m,
    u_shift,
    a_shift,
    b_shift,
    a_coef,
    inertia,
    strain,
    force,
    send_buf,
    recv_buf,
    u_slab,
    m_slab,
    v_slab,
    t_slab,
    f_slab,
    local_sem,
    send_sem,
    recv_sem,
):
    rows, cols, nz = mat_ref.shape
    wide_rows = rows + REACH
    gx = lax.axis_index("gx")
    gy = lax.axis_index("gy")
    place, _ = layout(rows, cols)
    listed = stages()
    number_of = {name: number for number, (name, _, _) in enumerate(listed)}

    def present(direction):
        x = gx + direction[0]
        y = gy + direction[1]
        return (x >= 0) & (x < grid_rows) & (y >= 0) & (y < grid_cols)

    here = {direction: present(direction) for direction in AROUND}

    barrier = pltpu.get_barrier_semaphore()
    for direction in AROUND:

        @pl.when(here[direction])
        def _(direction=direction):
            pl.semaphore_signal(
                barrier,
                inc=1,
                device_id=(gx + direction[0], gy + direction[1]),
                device_id_type=MESH,
            )

    loads = [
        pltpu.make_async_copy(source, target, local_sem.at[n])
        for n, (source, target) in enumerate(
            [
                (u_hbm, u_ref),
                (v_hbm, v_ref),
                (mat_hbm, mat_ref),
                (intact_hbm, intact_ref),
                (bulk_hbm, bulk_ref),
                (shear_hbm, shear_ref),
                (dens_hbm, dens_ref),
            ]
        )
    ]
    for load in loads:
        load.start()

    def side(value):
        return 0 if value < 0 else 1

    def slab(name, key):
        if name == "u":
            return u_slab
        if name == "m":
            return m_slab
        if name == "v":
            return v_slab
        buf = t_slab if name[0] == "t" else f_slab
        return buf.at[name[1], side(-key[1][0])]

    def ends(name, key, whole):
        number = number_of[name]
        if key[1][1] == 0:
            first = rows if key[0] == "C" else 0
            return whole.at[:, first : first + REACH], slab(name, key)
        at, size, _ = place[number, key]
        return send_buf.at[at : at + size], recv_buf.at[at : at + size]

    def copy_to(name, key, whole):
        dx, dy = key[1]
        source, target = ends(name, key, whole)
        return pltpu.make_async_remote_copy(
            src_ref=source,
            dst_ref=target,
            send_sem=send_sem.at[number_of[name], SLOT[key]],
            recv_sem=recv_sem.at[number_of[name], SLOT[key]],
            device_id=(gx + dx, gy + dy),
            device_id_type=MESH,
        )

    def pack(name, keys, whole, first_col):
        number = number_of[name]
        comps = listed[number][2]
        for key in keys:
            if key[1][1] == 0:
                continue
            at, _, runs = place[number, key]
            for comp in range(comps):
                for row, col, width in runs:
                    begin = first_col + col
                    send_buf[at : at + width] = whole[comp, row, begin : begin + width]
                    at += width

    def start_all(name, keys, whole):
        for key in keys:

            @pl.when(here[key[1]])
            def _(key=key):
                copy_to(name, key, whole).start()

    def wait_recv(name, key, whole):
        _, target = ends(name, key, whole)
        pltpu.make_async_remote_copy(
            src_ref=target,
            dst_ref=target,
            send_sem=send_sem.at[number_of[name], SLOT[key]],
            recv_sem=recv_sem.at[number_of[name], SLOT[key]],
            device_id=(gx - key[1][0], gy - key[1][1]),
            device_id_type=MESH,
        ).wait_recv()

    def wait_sends(name, keys, whole):
        for key in keys:

            @pl.when(here[key[1]])
            def _(key=key):
                copy_to(name, key, whole).wait_send()

    def landed(name, key):
        number = number_of[name]
        at, _, runs = place[number, key]
        dx, dy = key[1]
        for comp in range(listed[number][2]):
            for row, col, width in runs:
                yield comp, row - dx * rows, REACH + col - dy * cols, at, width
                at += width

    def take_state(name, keys, own, wide):
        for key in keys:
            origin = (-key[1][0], -key[1][1])

            @pl.when(here[origin])
            def _(key=key, origin=origin):
                wait_recv(name, key, own)
                if origin[1] == 0:
                    buf = slab(name, key)
                    for comp in range(own.shape[0]):
                        for r in range(REACH):
                            wide[comp, rows + r, REACH : REACH + cols] = buf[comp, r]
                    return
                for comp, row, col, at, width in landed(name, key):
                    wide[comp, row, col : col + width] = recv_buf[at : at + width]

    def take_sum(name, key, whole):
        origin = (-key[1][0], -key[1][1])

        @pl.when(here[origin])
        def _():
            wait_recv(name, key, whole)
            if origin[1] == 0:
                buf = slab(name, key)
                first = (rows if key[0] == "C" else 0) + origin[0] * rows
                for comp in range(whole.shape[0]):
                    for n in range(REACH):
                        whole[comp, first + n] = whole[comp, first + n] + buf[comp, n]
                return
            for comp, row, col, at, width in landed(name, key):
                span = slice(col, col + width)
                whole[comp, row, span] = whole[comp, row, span] + recv_buf[at : at + width]

    def take_sums(name, kind, whole, sent):
        order = ORDERS[kind]
        slabs = [key for key in keys_of(kind) if key[1][1] == 0]
        wait_sends(name, slabs, whole)
        if kind == "crossed":
            for key, late in zip(slabs, ("A late", "C late")):
                take_sum(name, key, whole)
                send_done(name, order, whole, late)
        else:
            for key in order["C"] + order["A"]:
                take_sum(name, key, whole)
        for other in sent:
            wait_sends(*other)
        if name == ("f", 0):
            take_state("v", STATE, v_ref, wide_v)
        for key in order["B"] + order["E"]:
            take_sum(name, key, whole)
        if kind == "crossed":
            for key in order["A late"]:
                take_sum(name, key, whole)

    def take_late(name, whole):
        for key in CROSSED["C late"]:
            take_sum(name, key, whole)

    loads[0].wait()
    pack("u", STATE, u_ref, 0)

    on_x = (gx > 0).astype(jnp.int32) + (gx < grid_rows - 1).astype(jnp.int32)
    on_y = (gy > 0).astype(jnp.int32) + (gy < grid_cols - 1).astype(jnp.int32)
    pl.semaphore_wait(barrier, (1 + on_x) * (1 + on_y) - 1)
    start_all("u", STATE, u_ref)

    loads[1].wait()
    loads[2].wait()
    mat_f32[0] = mat_ref[...].astype(F32)
    pack("m", STATE, mat_f32, 0)
    pack("v", STATE, v_ref, 0)

    wide_u[...] = jnp.zeros(wide_u.shape, F32)
    wide_v[...] = jnp.zeros(wide_v.shape, F32)
    wide_m[...] = jnp.zeros(wide_m.shape, F32)
    for comp in range(3):
        wide_u[comp, 0:rows, REACH : REACH + cols] = u_ref[comp]
        wide_v[comp, 0:rows, REACH : REACH + cols] = v_ref[comp]
    wide_m[0, 0:rows, REACH : REACH + cols] = mat_f32[0]

    def shifted(values, c):
        if c == 0:
            return values
        lane = lax.broadcasted_iota(jnp.int32, values.shape, 1)
        moved = pltpu.roll(values, (-c) % nz, axis=1)
        return jnp.where((lane + c >= 0) & (lane + c < nz), moved, 0.0)

    def shifts(r):
        return (0,) if r == wide_rows - 1 else range(-NEAR, NEAR + 1)

    def shift_motion(r):
        for comp in range(3):
            values = wide_u[comp, r]
            for c in shifts(r):
                moved = shifted(values, c)
                if comp == 2 and c != 0:
                    moved = moved + float(c)
                u_shift[c + NEAR, comp, r] = moved

    def advance(step, r):
        for comp in range(3):
            speed = wide_v[comp, r] + force[step, comp, r] * inertia[r]
            wide_v[comp, r] = speed
            wide_u[comp, r] = wide_u[comp, r] + TIME_STEP * speed
        shift_motion(r)

    def shift_pressure(step, r):
        values = strain[step, 0, r] * a_coef[r]
        for c in shifts(r):
            a_shift[c + NEAR, r] = shifted(values, c)

    def just_in_time(make):
        made = set()

        def need(i, groups):
            for r in sorted({i} | {i + a for a, _ in groups}):
                if r not in made:
                    made.add(r)
                    make(r)

        return need

    def materials():
        for r in range(wide_rows):
            classes = wide_m[0, r]
            bulk = jnp.full(classes.shape, bulk_ref[0], F32)
            shear = jnp.full(classes.shape, shear_ref[0], F32)
            dens = jnp.full(classes.shape, dens_ref[0], F32)
            for number in range(1, bulk_ref.shape[0]):
                match = classes == float(number)
                bulk = jnp.where(match, bulk_ref[number], bulk)
                shear = jnp.where(match, shear_ref[number], shear)
                dens = jnp.where(match, dens_ref[number], dens)
            inertia[r] = TIME_STEP / dens
            a_coef[r] = (9.0 / (VOLUME * VOLUME)) * (bulk - (5.0 / 3.0) * shear)
            stiff = (15.0 / VOLUME) * shear
            for c in shifts(r):
                b_shift[c + NEAR, r] = shifted(stiff, c)

    depth = lax.broadcasted_iota(jnp.int32, (cols, nz), 1)
    column = lax.broadcasted_iota(jnp.int32, (cols, nz), 0) + gy * cols

    def partner(buffer, i, a, b, c, own):
        if c > NEAR:
            return shifted(own, c)
        return buffer[c + NEAR, i + a, pl.ds(REACH + b, cols)]

    def bond_vector(i, a, b, c, own):
        y = []
        for comp in range(3):
            if c > NEAR:
                there = shifted(own[3][comp], c)
                if comp == 2:
                    there = there + float(c)
            else:
                there = u_shift[c + NEAR, comp, i + a, pl.ds(REACH + b, cols)]
            y.append(there - (own[0][a], own[1][b], own[2])[comp])
        return y

    def geometry(i, a, b, c, own):
        y0, y1, y2 = bond_vector(i, a, b, c, own)
        square = y0 * y0 + y1 * y1 + y2 * y2
        inverse = lax.rsqrt(square)
        return square * inverse, inverse

    def own_motion(i):
        mine = [wide_u[comp, i, REACH : REACH + cols] for comp in range(3)]
        by_row = {a: mine[0] - float(a) for a in range(REACH + 1)}
        by_col = {b: mine[1] - float(b) for b in range(-REACH, REACH + 1)}
        return (by_row, by_col, mine[2], mine)

    def back(values, c):
        return values if c == 0 else pltpu.roll(values, c % nz, axis=1)

    def packed_of(name, kind, whole):
        return [(name, [key for key in keys_of(kind) if key[1][1] != 0], whole)]

    def send_done(name, keys, whole, chunk):
        pack(name, keys[chunk], whole, REACH)
        start_all(name, keys[chunk], whole)

    def weights():
        @pl.loop(0, rows)
        def _(i):
            lane_in = {
                c: jnp.where((depth + c >= 0) & (depth + c < nz), 1.0, 0.0)
                for c in range(-NEAR, REACH + 1)
            }
            for (a, b), members in GROUPS.items():
                row_in = (gx * rows + i + a) < grid_rows * rows
                plane = jnp.where(
                    (column + b >= 0) & (column + b < grid_cols * cols) & row_in, 1.0, 0.0
                )
                for k, c in members:
                    flag[k, i] = intact_ref[k, i].astype(F32) * (plane * lane_in[c])

    def prepare():
        @pl.loop(0, rows)
        def _(i):
            own_b = b_shift[NEAR, i, pl.ds(REACH, cols)]
            for k, (a, b, c) in enumerate(OFFSETS):
                both_b = own_b + partner(b_shift, i, a, b, c, own_b)
                scale = flag[k, i] * by_inverse[k, i]
                by_stretch[k, i] = scale * (both_b * (by_stretch[k, i] * (1.0 / RADII[k])))
                by_inverse[k, i] = scale

    def strain_pass(sums_ref, need, send, far_rows):
        mid = pl.ds(REACH, cols)
        for chunk, work in bond_order(rows, "ABCE"):
            if chunk == "C":
                far_rows()
            for i, groups in work:
                need(i, groups)
                own = own_motion(i)
                sums = []
                for a, b in groups:
                    returned = []
                    for k, c in GROUPS[a, b]:
                        length, inverse = geometry(i, a, b, c, own)
                        stretch = length - RADII[k]
                        by_inverse[k, i] = inverse
                        by_stretch[k, i] = stretch
                        term = flag[k, i] * stretch
                        sums.append(term)
                        returned.append(back(term, c))
                    at = pl.ds(REACH + b, cols)
                    sums_ref[0, i + a, at] = sums_ref[0, i + a, at] + tree_sum(returned)
                    sums = [tree_sum(sums)]
                sums_ref[0, i, mid] = sums_ref[0, i, mid] + sums[0]
            send(chunk)

    def tensions_of(i, a, b, own_a):
        found = []
        for k, c in GROUPS[a, b]:
            both_a = own_a + partner(a_shift, i, a, b, c, own_a)
            found.append((c, by_inverse[k, i] * both_a + by_stretch[k, i]))
        return found

    def pull_origin(i, a, b, tensions, own):
        at = pl.ds(REACH + b, cols)
        base = (own[0][a], own[1][b], own[2])
        total = tree_sum([tension for _, tension in tensions])
        return [
            tree_sum([t * u_shift[c + NEAR, comp, i + a, at] for c, t in tensions])
            - base[comp] * total
            for comp in range(3)
        ]

    def pull_partner(i, a, b, tensions, sums_ref):
        mid = pl.ds(REACH, cols)
        at = pl.ds(REACH + b, cols)
        pulled = [(c, back(tension, c)) for c, tension in tensions]
        total = tree_sum([tension for _, tension in pulled])
        for comp, shift in enumerate((float(a), float(b), 0.0)):
            origin = tree_sum([t * u_shift[NEAR - c, comp, i, mid] for c, t in pulled])
            end = u_shift[NEAR, comp, i + a, at] + shift
            sums_ref[comp, i + a, at] = sums_ref[comp, i + a, at] + (origin - end * total)

    def pull_both(i, a, b, tensions, own, sums_ref, sums):
        at = pl.ds(REACH + b, cols)
        returned = [[], [], []]
        for c, tension in tensions:
            y = bond_vector(i, a, b, c, own)
            for comp in range(3):
                term = tension * y[comp]
                sums[comp].append(term)
                returned[comp].append(back(term, c))
        for comp in range(3):
            sums_ref[comp, i + a, at] = sums_ref[comp, i + a, at] - tree_sum(returned[comp])

    def force_pass(sums_ref, need, send):
        mid = pl.ds(REACH, cols)
        for chunk, work in bond_order(rows, "CABE"):
            for i, groups in work:
                need(i, groups)
                own = own_motion(i)
                own_a = a_shift[NEAR, i, mid]
                sums = [[], [], []]
                for a, b in groups:
                    tensions = tensions_of(i, a, b, own_a)
                    if (a, b) in AT_PARTNER:
                        for comp, part in enumerate(pull_origin(i, a, b, tensions, own)):
                            sums[comp].append(part)
                        pull_partner(i, a, b, tensions, sums_ref)
                    else:
                        pull_both(i, a, b, tensions, own, sums_ref, sums)
                    sums = [[tree_sum(sums[comp])] for comp in range(3)]
                for comp in range(3):
                    sums_ref[comp, i, mid] = sums_ref[comp, i, mid] + sums[comp][0]
            send(chunk)

    def last_force_pass(sums_ref, need, send):
        mid = pl.ds(REACH, cols)
        for chunk, work in bond_order(rows, "CABE"):
            for i, groups in work:
                leaving = [(a, b) for a, b in groups if b != 0 or i + a >= rows]
                need(i, groups)
                own_a = a_shift[NEAR, i, mid]
                for a, b in leaving:
                    tensions = tensions_of(i, a, b, own_a)
                    for (k, _), (_, tension) in zip(GROUPS[a, b], tensions):
                        by_stretch[k, i] = tension
                    pull_partner(i, a, b, tensions, sums_ref)
            send(chunk)
        for i in range(rows):
            own = own_motion(i)
            own_a = a_shift[NEAR, i, mid]
            sums = [[], [], []]
            for a, b in GROUPS:
                if b != 0 or i + a >= rows:
                    tensions = [(c, by_stretch[k, i]) for k, c in GROUPS[a, b]]
                    for comp, part in enumerate(pull_origin(i, a, b, tensions, own)):
                        sums[comp].append(part)
                else:
                    tensions = tensions_of(i, a, b, own_a)
                    pull_both(i, a, b, tensions, own, sums_ref, sums)
                sums = [[tree_sum(sums[comp])] for comp in range(3)]
            for comp in range(3):
                sums_ref[comp, i, mid] = sums_ref[comp, i, mid] + sums[comp][0]

    for load in loads[3:]:
        load.wait()
    weights()
    strain[...] = jnp.zeros(strain.shape, F32)
    force[...] = jnp.zeros(force.shape, F32)
    take_state("u", [key for key in STATE if key[1][0] == 0], u_ref, wide_u)
    start_all("m", STATE, mat_f32)

    sent = [("u", STATE, u_ref)]
    for step in range(STEPS):
        last = step == STEPS - 1
        name = ("t", step)
        whole = strain.at[step]
        if step == 0:
            make = shift_motion
            far = [key for key in STATE if key[1][0] != 0]
            far_rows = functools.partial(take_state, "u", far, u_ref, wide_u)
        else:
            make = functools.partial(advance, step - 1)
            far_rows = functools.partial(take_late, ("f", step - 1), force.at[step - 1])
        strain_pass(
            whole, just_in_time(make), functools.partial(send_done, name, CHUNKS, whole), far_rows
        )
        if step == 0:
            start_all("v", STATE, v_ref)
            take_state("m", STATE, mat_f32, wide_m)
            materials()
        prepare()
        take_sums(name, "sum", whole, sent)
        sent = packed_of(name, "sum", whole)
        if step == 0:
            sent = sent + [("m", STATE, mat_f32), ("v", STATE, v_ref)]

        name = ("f", step)
        whole = force.at[step]
        kind = "final" if last else "crossed"
        run = last_force_pass if last else force_pass
        run(
            whole,
            just_in_time(functools.partial(shift_pressure, step)),
            functools.partial(send_done, name, ORDERS[kind], whole),
        )
        packed_now = packed_of(name, kind, whole)
        take_sums(name, kind, whole, sent + packed_now if last else sent)
        sent = packed_now
        if last:
            mid = pl.ds(REACH, cols)
            for r in range(rows):
                for comp in range(3):
                    pull = force[step, comp, r, mid]
                    speed = wide_v[comp, r, mid] + pull * inertia[r, mid]
                    out_f[comp, r] = pull
                    out_v[comp, r] = speed
                    out_u[comp, r] = wide_u[comp, r, mid] + TIME_STEP * speed


def hand_over(u_in, v_in, f_in, u_out, v_out, f_out):
    u_out[...] = u_in[...]
    v_out[...] = v_in[...]
    f_out[...] = f_in[...]


def on_device(displacement, velocity, intact, material, bulk_modulus, shear_modulus, density):
    rows, cols, nz = material.shape
    wide_rows = rows + REACH
    padded = round_up(cols + 2 * REACH, 8)
    packed = layout(rows, cols)[1]
    own = jax.ShapeDtypeStruct((3, rows, cols, nz), F32)
    vmem = pl.BlockSpec(memory_space=pltpu.VMEM)
    hbm = pl.BlockSpec(memory_space=pltpu.HBM)
    table = pltpu.SMEM(bulk_modulus.shape, F32)

    def buffer(*shape):
        return pltpu.VMEM(shape + (nz,), F32)

    results = pl.pallas_call(
        functools.partial(kernel, lax.axis_size("gx"), lax.axis_size("gy")),
        out_shape=(own, own, own),
        in_specs=[hbm] * 7,
        out_specs=(vmem, vmem, vmem),
        scratch_shapes=[
            buffer(3, rows, cols),
            buffer(3, rows, cols),
            pltpu.VMEM(material.shape, jnp.int32),
            buffer(1, rows, cols),
            table,
            table,
            table,
            pltpu.VMEM(intact.shape, jnp.int32),
            pltpu.VMEM(intact.shape, F32),
            pltpu.VMEM(intact.shape, F32),
            pltpu.VMEM(intact.shape, F32),
            buffer(3, wide_rows, padded),
            buffer(3, wide_rows, padded),
            buffer(1, wide_rows, padded),
            buffer(5, 3, wide_rows, padded),
            buffer(5, wide_rows, padded),
            buffer(5, wide_rows, padded),
            buffer(wide_rows, padded),
            buffer(wide_rows, padded),
            buffer(STEPS, 1, wide_rows, padded),
            buffer(STEPS, 3, wide_rows, padded),
            buffer(packed),
            buffer(packed),
            buffer(3, REACH, cols),
            buffer(1, REACH, cols),
            buffer(3, REACH, cols),
            buffer(STEPS, 2, 1, REACH, padded),
            buffer(STEPS, 2, 3, REACH, padded),
            pltpu.SemaphoreType.DMA((7,)),
            pltpu.SemaphoreType.DMA((len(stages()), SLOTS)),
            pltpu.SemaphoreType.DMA((len(stages()), SLOTS)),
        ],
        compiler_params=pltpu.CompilerParams(
            collective_id=0, has_side_effects=True, vmem_limit_bytes=67_043_328
        ),
        name="peridynamics",
    )(displacement, velocity, intact, material, bulk_modulus, shear_modulus, density)
    return pl.pallas_call(
        hand_over,
        out_shape=(own, own, own),
        in_specs=[vmem] * 3,
        out_specs=(vmem, vmem, vmem),
        name="hand_over",
    )(*results)


def solution(mesh):
    node = P(None, "gx", "gy", None)
    return jax.shard_map(
        on_device,
        mesh=mesh,
        in_specs=(node, node, node, P("gx", "gy", None), P(), P(), P()),
        out_specs=(node, node, node),
        check_vma=False,
    )
```

```python
import functools
import math

import jax
import jax.numpy as jnp
from jax import lax
from jax.experimental import pallas as pl
from jax.experimental.pallas import tpu as pltpu
from jax.sharding import PartitionSpec as P

STEPS = 2
TIME_STEP = 0.02
REACH = 3
NEAR = 2
MESH = pl.DeviceIdType.MESH
F32 = jnp.float32

AROUND = [(dx, dy) for dx in (-1, 0, 1) for dy in (-1, 0, 1) if (dx, dy) != (0, 0)]
STATE = [("S", (-1, 0)), ("S", (0, -1)), ("S", (0, 1)), ("S", (-1, -1)), ("S", (-1, 1))]
CHUNKS = {
    "C": [("C", (1, -1)), ("C", (1, 1)), ("C", (0, -1)), ("C", (0, 1)), ("C", (1, 0))],
    "A": [("A", (-1, -1)), ("A", (-1, 1)), ("A", (0, -1)), ("A", (0, 1)), ("A", (-1, 0))],
    "B": [("B", (0, -1)), ("B", (0, 1))],
    "E": [("E", (0, -1)), ("E", (0, 1))],
}
FINAL = {
    "C": [("C", (1, -1)), ("C", (1, 1)), ("C", (1, 0))],
    "A": [("A", (0, -1)), ("A", (0, 1))],
    "B": [("B", (0, -1)), ("B", (0, 1))],
    "E": [("E", (0, -1)), ("E", (0, 1))],
}
CROSSED = {
    "C": [("C", (1, 0))],
    "A": [("A", (-1, 0))],
    "B": [("B", (0, -1)), ("B", (0, 1))],
    "E": [("E", (0, -1)), ("E", (0, 1))],
    "A late": [("A", (0, -1)), ("A", (0, 1))],
    "C late": [("C", (0, -1)), ("C", (0, 1))],
}
ORDERS = {"sum": CHUNKS, "final": FINAL, "crossed": CROSSED}
SLOT = {key: n for n, key in enumerate(sum(CHUNKS.values(), []))}
SLOTS = len(SLOT)
SLOT.update({key: n for n, key in enumerate(STATE)})


def half_offsets():
    span = range(-REACH, REACH + 1)
    return [
        (a, b, c)
        for a in span
        for b in span
        for c in span
        if a * a + b * b + c * c <= REACH * REACH and (a, b, c) > (0, 0, 0)
    ]


OFFSETS = half_offsets()
GROUPS = {}
for _k, (_a, _b, _c) in enumerate(OFFSETS):
    GROUPS.setdefault((_a, _b), []).append((_k, _c))
RADII = [math.sqrt(float(a * a + b * b + c * c)) for a, b, c in OFFSETS]
VOLUME = 2.0 * sum(RADII)


def round_up(value, unit):
    return -(-value // unit) * unit


AT_PARTNER = [(a, b) for a in (1, 2) for b in (-2, -1, 1, 2)]


def bond_order(rows, order):
    tail = range(rows - REACH, rows)
    groups = list(GROUPS)
    work = {
        "C": [(i, [(a, b) for a, b in groups if i + a >= rows]) for i in tail],
        "A": [(i, groups) for i in range(REACH)],
        "B": [(i, groups) for i in range(REACH, rows - REACH)],
        "E": [(i, [(a, b) for a, b in groups if i + a < rows]) for i in tail],
    }
    return [(chunk, work[chunk]) for chunk in order]


def spans(rows, cols, key, kind):
    chunk, (dx, dy) = key
    own = {(r, c) for r in range(rows) for c in range(cols)}
    wide = own | {(r + a, c + b) for r, c in own for a, b in GROUPS}
    sender = own if kind == "state" else wide
    if kind == "crossed":
        sender = {(r + x, c) for r, c in wide for x in (-rows, 0, rows)}
    receiver = own if kind == "final" else wide
    first, end = {
        "A": (0, REACH),
        "B": (REACH, rows - REACH),
        "E": (rows - REACH, rows),
        "C": (rows, rows + REACH),
        "S": (0, rows),
    }[chunk]
    runs = []
    for row in range(first, end):
        used = [c for r, c in sender if r == row and (r - dx * rows, c - dy * cols) in receiver]
        if used:
            runs.append((row, min(used), max(used) + 1 - min(used)))
    return runs


def stages():
    listed = [("u", "state", 3), ("m", "state", 1), ("v", "state", 3)]
    for step in range(STEPS):
        listed.append((("t", step), "sum", 1))
        listed.append((("f", step), "final" if step == STEPS - 1 else "crossed", 3))
    return listed


def keys_of(kind):
    if kind == "state":
        return STATE
    return sum(ORDERS[kind].values(), [])


def layout(rows, cols):
    place, at = {}, 0
    for number, (_, kind, comps) in enumerate(stages()):
        for key in keys_of(kind):
            if key[1][1] == 0:
                continue
            runs = spans(rows, cols, key, kind)
            size = round_up(comps * sum(width for _, _, width in runs), 8)
            place[number, key] = (at, size, runs)
            at += size
    return place, at


def tree_sum(terms):
    while len(terms) > 1:
        terms = [
            terms[n] + terms[n + 1] if n + 1 < len(terms) else terms[n]
            for n in range(0, len(terms), 2)
        ]
    return terms[0]


def kernel(
    grid_rows,
    grid_cols,
    u_hbm,
    v_hbm,
    intact_hbm,
    mat_hbm,
    bulk_hbm,
    shear_hbm,
    dens_hbm,
    out_u,
    out_v,
    out_f,
    u_ref,
    v_ref,
    mat_ref,
    mat_f32,
    bulk_ref,
    shear_ref,
    dens_ref,
    intact_ref,
    flag,
    by_inverse,
    by_stretch,
    wide_u,
    wide_v,
    wide_m,
    u_shift,
    a_shift,
    b_shift,
    a_coef,
    inertia,
    strain,
    force,
    send_buf,
    recv_buf,
    u_slab,
    m_slab,
    v_slab,
    t_slab,
    f_slab,
    local_sem,
    send_sem,
    recv_sem,
):
    rows, cols, nz = mat_ref.shape
    wide_rows = rows + REACH
    gx = lax.axis_index("gx")
    gy = lax.axis_index("gy")
    place, _ = layout(rows, cols)
    listed = stages()
    number_of = {name: number for number, (name, _, _) in enumerate(listed)}

    def present(direction):
        x = gx + direction[0]
        y = gy + direction[1]
        return (x >= 0) & (x < grid_rows) & (y >= 0) & (y < grid_cols)

    here = {direction: present(direction) for direction in AROUND}

    barrier = pltpu.get_barrier_semaphore()
    for direction in AROUND:

        @pl.when(here[direction])
        def _(direction=direction):
            pl.semaphore_signal(
                barrier,
                inc=1,
                device_id=(gx + direction[0], gy + direction[1]),
                device_id_type=MESH,
            )

    loads = [
        pltpu.make_async_copy(source, target, local_sem.at[n])
        for n, (source, target) in enumerate(
            [
                (u_hbm, u_ref),
                (v_hbm, v_ref),
                (mat_hbm, mat_ref),
                (intact_hbm, intact_ref),
                (bulk_hbm, bulk_ref),
                (shear_hbm, shear_ref),
                (dens_hbm, dens_ref),
            ]
        )
    ]
    for load in loads:
        load.start()

    def side(value):
        return 0 if value < 0 else 1

    def slab(name, key):
        if name == "u":
            return u_slab
        if name == "m":
            return m_slab
        if name == "v":
            return v_slab
        buf = t_slab if name[0] == "t" else f_slab
        return buf.at[name[1], side(-key[1][0])]

    def ends(name, key, whole):
        number = number_of[name]
        if key[1][1] == 0:
            first = rows if key[0] == "C" else 0
            return whole.at[:, first : first + REACH], slab(name, key)
        at, size, _ = place[number, key]
        return send_buf.at[at : at + size], recv_buf.at[at : at + size]

    def copy_to(name, key, whole):
        dx, dy = key[1]
        source, target = ends(name, key, whole)
        return pltpu.make_async_remote_copy(
            src_ref=source,
            dst_ref=target,
            send_sem=send_sem.at[number_of[name], SLOT[key]],
            recv_sem=recv_sem.at[number_of[name], SLOT[key]],
            device_id=(gx + dx, gy + dy),
            device_id_type=MESH,
        )

    def pack(name, keys, whole, first_col):
        number = number_of[name]
        comps = listed[number][2]
        for key in keys:
            if key[1][1] == 0:
                continue
            at, _, runs = place[number, key]
            for comp in range(comps):
                for row, col, width in runs:
                    begin = first_col + col
                    send_buf[at : at + width] = whole[comp, row, begin : begin + width]
                    at += width

    def start_all(name, keys, whole):
        for key in keys:

            @pl.when(here[key[1]])
            def _(key=key):
                copy_to(name, key, whole).start()

    def wait_recv(name, key, whole):
        _, target = ends(name, key, whole)
        pltpu.make_async_remote_copy(
            src_ref=target,
            dst_ref=target,
            send_sem=send_sem.at[number_of[name], SLOT[key]],
            recv_sem=recv_sem.at[number_of[name], SLOT[key]],
            device_id=(gx - key[1][0], gy - key[1][1]),
            device_id_type=MESH,
        ).wait_recv()

    def wait_sends(name, keys, whole):
        for key in keys:

            @pl.when(here[key[1]])
            def _(key=key):
                copy_to(name, key, whole).wait_send()

    def landed(name, key):
        number = number_of[name]
        at, _, runs = place[number, key]
        dx, dy = key[1]
        for comp in range(listed[number][2]):
            for row, col, width in runs:
                yield comp, row - dx * rows, REACH + col - dy * cols, at, width
                at += width

    def take_state(name, keys, own, wide):
        for key in keys:
            origin = (-key[1][0], -key[1][1])

            @pl.when(here[origin])
            def _(key=key, origin=origin):
                wait_recv(name, key, own)
                if origin[1] == 0:
                    buf = slab(name, key)
                    for comp in range(own.shape[0]):
                        for r in range(REACH):
                            wide[comp, rows + r, REACH : REACH + cols] = buf[comp, r]
                    return
                for comp, row, col, at, width in landed(name, key):
                    wide[comp, row, col : col + width] = recv_buf[at : at + width]

    def take_sum(name, key, whole):
        origin = (-key[1][0], -key[1][1])

        @pl.when(here[origin])
        def _():
            wait_recv(name, key, whole)
            if origin[1] == 0:
                buf = slab(name, key)
                first = (rows if key[0] == "C" else 0) + origin[0] * rows
                for comp in range(whole.shape[0]):
                    for n in range(REACH):
                        whole[comp, first + n] = whole[comp, first + n] + buf[comp, n]
                return
            for comp, row, col, at, width in landed(name, key):
                span = slice(col, col + width)
                whole[comp, row, span] = whole[comp, row, span] + recv_buf[at : at + width]

    def take_sums(name, kind, whole, sent):
        order = ORDERS[kind]
        slabs = [key for key in keys_of(kind) if key[1][1] == 0]
        wait_sends(name, slabs, whole)
        if kind == "crossed":
            for key, late in zip(slabs, ("A late", "C late")):
                take_sum(name, key, whole)
                send_done(name, order, whole, late)
        else:
            for key in order["C"] + order["A"]:
                take_sum(name, key, whole)
        for other in sent:
            wait_sends(*other)
        if name == ("f", 0):
            take_state("v", STATE, v_ref, wide_v)
        for key in order["B"] + order["E"]:
            take_sum(name, key, whole)

    def take_late(name, whole, chunk):
        for key in CROSSED[chunk + " late"]:
            take_sum(name, key, whole)

    loads[0].wait()
    pack("u", STATE, u_ref, 0)
    loads[2].wait()
    mat_f32[0] = mat_ref[...].astype(F32)
    pack("m", STATE, mat_f32, 0)

    on_x = (gx > 0).astype(jnp.int32) + (gx < grid_rows - 1).astype(jnp.int32)
    on_y = (gy > 0).astype(jnp.int32) + (gy < grid_cols - 1).astype(jnp.int32)
    pl.semaphore_wait(barrier, (1 + on_x) * (1 + on_y) - 1)
    start_all("u", STATE, u_ref)

    loads[1].wait()
    pack("v", STATE, v_ref, 0)

    wide_u[...] = jnp.zeros(wide_u.shape, F32)
    wide_v[...] = jnp.zeros(wide_v.shape, F32)
    wide_m[...] = jnp.zeros(wide_m.shape, F32)
    for comp in range(3):
        wide_u[comp, 0:rows, REACH : REACH + cols] = u_ref[comp]
        wide_v[comp, 0:rows, REACH : REACH + cols] = v_ref[comp]
    wide_m[0, 0:rows, REACH : REACH + cols] = mat_f32[0]

    def shifted(values, c):
        if c == 0:
            return values
        lane = lax.broadcasted_iota(jnp.int32, values.shape, 1)
        moved = pltpu.roll(values, (-c) % nz, axis=1)
        return jnp.where((lane + c >= 0) & (lane + c < nz), moved, 0.0)

    def shifts(r):
        return (0,) if r == wide_rows - 1 else range(-NEAR, NEAR + 1)

    def shift_motion(r):
        for comp in range(3):
            values = wide_u[comp, r]
            for c in shifts(r):
                moved = shifted(values, c)
                if comp == 2 and c != 0:
                    moved = moved + float(c)
                u_shift[c + NEAR, comp, r] = moved

    def advance(step, r):
        for comp in range(3):
            speed = wide_v[comp, r] + force[step, comp, r] * inertia[r]
            wide_v[comp, r] = speed
            wide_u[comp, r] = wide_u[comp, r] + TIME_STEP * speed
        shift_motion(r)

    def shift_pressure(step, r):
        values = strain[step, 0, r] * a_coef[r]
        for c in shifts(r):
            a_shift[c + NEAR, r] = shifted(values, c)

    def just_in_time(make):
        made = set()

        def need(i, groups):
            for r in sorted({i} | {i + a for a, _ in groups}):
                if r not in made:
                    made.add(r)
                    make(r)

        return need

    def materials():
        for r in range(wide_rows):
            classes = wide_m[0, r]
            bulk = jnp.full(classes.shape, bulk_ref[0], F32)
            shear = jnp.full(classes.shape, shear_ref[0], F32)
            dens = jnp.full(classes.shape, dens_ref[0], F32)
            for number in range(1, bulk_ref.shape[0]):
                match = classes == float(number)
                bulk = jnp.where(match, bulk_ref[number], bulk)
                shear = jnp.where(match, shear_ref[number], shear)
                dens = jnp.where(match, dens_ref[number], dens)
            inertia[r] = TIME_STEP / dens
            a_coef[r] = (9.0 / (VOLUME * VOLUME)) * (bulk - (5.0 / 3.0) * shear)
            stiff = (15.0 / VOLUME) * shear
            for c in shifts(r):
                b_shift[c + NEAR, r] = shifted(stiff, c)

    depth = lax.broadcasted_iota(jnp.int32, (cols, nz), 1)
    column = lax.broadcasted_iota(jnp.int32, (cols, nz), 0) + gy * cols

    def partner(buffer, i, a, b, c, own):
        if c > NEAR:
            return shifted(own, c)
        return buffer[c + NEAR, i + a, pl.ds(REACH + b, cols)]

    def bond_vector(i, a, b, c, own):
        y = []
        for comp in range(3):
            if c > NEAR:
                there = shifted(own[3][comp], c)
                if comp == 2:
                    there = there + float(c)
            else:
                there = u_shift[c + NEAR, comp, i + a, pl.ds(REACH + b, cols)]
            y.append(there - (own[0][a], own[1][b], own[2])[comp])
        return y

    def geometry(i, a, b, c, own):
        y0, y1, y2 = bond_vector(i, a, b, c, own)
        square = y0 * y0 + y1 * y1 + y2 * y2
        inverse = lax.rsqrt(square)
        return square * inverse, inverse

    def own_motion(i):
        mine = [wide_u[comp, i, REACH : REACH + cols] for comp in range(3)]
        by_row = {a: mine[0] - float(a) for a in range(REACH + 1)}
        by_col = {b: mine[1] - float(b) for b in range(-REACH, REACH + 1)}
        return (by_row, by_col, mine[2], mine)

    def back(values, c):
        return values if c == 0 else pltpu.roll(values, c % nz, axis=1)

    def packed_of(name, kind, whole):
        return [(name, [key for key in keys_of(kind) if key[1][1] != 0], whole)]

    def send_done(name, keys, whole, chunk):
        pack(name, keys[chunk], whole, REACH)
        start_all(name, keys[chunk], whole)

    def weights():
        @pl.loop(0, rows)
        def _(i):
            lane_in = {
                c: jnp.where((depth + c >= 0) & (depth + c < nz), 1.0, 0.0)
                for c in range(-NEAR, REACH + 1)
            }
            for (a, b), members in GROUPS.items():
                row_in = (gx * rows + i + a) < grid_rows * rows
                plane = jnp.where(
                    (column + b >= 0) & (column + b < grid_cols * cols) & row_in, 1.0, 0.0
                )
                for k, c in members:
                    flag[k, i] = intact_ref[k, i].astype(F32) * (plane * lane_in[c])

    def prepare():
        @pl.loop(0, rows)
        def _(i):
            own_b = b_shift[NEAR, i, pl.ds(REACH, cols)]
            for k, (a, b, c) in enumerate(OFFSETS):
                both_b = own_b + partner(b_shift, i, a, b, c, own_b)
                scale = flag[k, i] * by_inverse[k, i]
                by_stretch[k, i] = scale * (both_b * (by_stretch[k, i] * (1.0 / RADII[k])))
                by_inverse[k, i] = scale

    def stays(i, a, b):
        return b == 0 and i + a < rows

    def strain_pass(sums_ref, order, need, arrive, send):
        mid = pl.ds(REACH, cols)
        for chunk, work in order:
            arrive(chunk)
            for i, groups in work:
                need(i, groups)
                own = own_motion(i)
                sums = []
                for a, b in groups:
                    returned = []
                    for k, c in GROUPS[a, b]:
                        length, inverse = geometry(i, a, b, c, own)
                        stretch = length - RADII[k]
                        by_inverse[k, i] = inverse
                        by_stretch[k, i] = stretch
                        term = flag[k, i] * stretch
                        sums.append(term)
                        returned.append(back(term, c))
                    at = pl.ds(REACH + b, cols)
                    sums_ref[0, i + a, at] = sums_ref[0, i + a, at] + tree_sum(returned)
                    sums = [tree_sum(sums)]
                sums_ref[0, i, mid] = sums_ref[0, i, mid] + sums[0]
            send(chunk)

    def tensions_of(i, a, b, own_a):
        found = []
        for k, c in GROUPS[a, b]:
            both_a = own_a + partner(a_shift, i, a, b, c, own_a)
            found.append((c, by_inverse[k, i] * both_a + by_stretch[k, i]))
        return found

    def pull_origin(i, a, b, tensions, own):
        at = pl.ds(REACH + b, cols)
        base = (own[0][a], own[1][b], own[2])
        total = tree_sum([tension for _, tension in tensions])
        return [
            tree_sum([t * u_shift[c + NEAR, comp, i + a, at] for c, t in tensions])
            - base[comp] * total
            for comp in range(3)
        ]

    def pull_partner(i, a, b, tensions, sums_ref):
        mid = pl.ds(REACH, cols)
        at = pl.ds(REACH + b, cols)
        pulled = [(c, back(tension, c)) for c, tension in tensions]
        total = tree_sum([tension for _, tension in pulled])
        for comp, shift in enumerate((float(a), float(b), 0.0)):
            origin = tree_sum([t * u_shift[NEAR - c, comp, i, mid] for c, t in pulled])
            end = u_shift[NEAR, comp, i + a, at] + shift
            sums_ref[comp, i + a, at] = sums_ref[comp, i + a, at] + (origin - end * total)

    def pull_both(i, a, b, tensions, own, sums_ref, sums):
        at = pl.ds(REACH + b, cols)
        returned = [[], [], []]
        for c, tension in tensions:
            y = bond_vector(i, a, b, c, own)
            for comp in range(3):
                term = tension * y[comp]
                sums[comp].append(term)
                returned[comp].append(back(term, c))
        for comp in range(3):
            sums_ref[comp, i + a, at] = sums_ref[comp, i + a, at] - tree_sum(returned[comp])

    def force_pass(sums_ref, need, send):
        mid = pl.ds(REACH, cols)
        for chunk, work in bond_order(rows, "CABE"):
            for i, groups in work:
                need(i, groups)
                own = own_motion(i)
                own_a = a_shift[NEAR, i, mid]
                sums = [[], [], []]
                for a, b in groups:
                    tensions = tensions_of(i, a, b, own_a)
                    if (a, b) in AT_PARTNER:
                        for comp, part in enumerate(pull_origin(i, a, b, tensions, own)):
                            sums[comp].append(part)
                        pull_partner(i, a, b, tensions, sums_ref)
                    else:
                        pull_both(i, a, b, tensions, own, sums_ref, sums)
                    sums = [[tree_sum(sums[comp])] for comp in range(3)]
                for comp in range(3):
                    sums_ref[comp, i, mid] = sums_ref[comp, i, mid] + sums[comp][0]
            send(chunk)

    def last_force_pass(sums_ref, need, send):
        mid = pl.ds(REACH, cols)
        for chunk, work in bond_order(rows, "CABE"):
            for i, groups in work:
                leaving = [(a, b) for a, b in groups if b != 0 or i + a >= rows]
                need(i, groups)
                own_a = a_shift[NEAR, i, mid]
                for a, b in leaving:
                    tensions = tensions_of(i, a, b, own_a)
                    for (k, _), (_, tension) in zip(GROUPS[a, b], tensions):
                        by_stretch[k, i] = tension
                    pull_partner(i, a, b, tensions, sums_ref)
            send(chunk)
        for i in range(rows):
            own = own_motion(i)
            own_a = a_shift[NEAR, i, mid]
            sums = [[], [], []]
            for a, b in GROUPS:
                if b != 0 or i + a >= rows:
                    tensions = [(c, by_stretch[k, i]) for k, c in GROUPS[a, b]]
                    for comp, part in enumerate(pull_origin(i, a, b, tensions, own)):
                        sums[comp].append(part)
                else:
                    tensions = tensions_of(i, a, b, own_a)
                    pull_both(i, a, b, tensions, own, sums_ref, sums)
                sums = [[tree_sum(sums[comp])] for comp in range(3)]
            for comp in range(3):
                sums_ref[comp, i, mid] = sums_ref[comp, i, mid] + sums[comp][0]

    for load in loads[3:]:
        load.wait()
    weights()
    strain[...] = jnp.zeros(strain.shape, F32)
    force[...] = jnp.zeros(force.shape, F32)
    start_all("m", STATE, mat_f32)

    def near(i, groups):
        return [(a, b) for a, b in groups if stays(i, a, b)]

    def rest(i, groups):
        return [(a, b) for a, b in groups if not stays(i, a, b)]

    strain_pass(
        strain.at[0],
        [("", [(i, near(i, GROUPS)) for i in range(rows)])],
        just_in_time(shift_motion),
        lambda chunk: None,
        lambda chunk: None,
    )
    take_state("u", [key for key in STATE if key[1][0] == 0], u_ref, wide_u)

    sent = [("u", STATE, u_ref)]
    for step in range(STEPS):
        last = step == STEPS - 1
        name = ("t", step)
        whole = strain.at[step]
        if step == 0:
            make = shift_motion
            order = [
                (chunk, [(i, rest(i, groups)) for i, groups in work])
                for chunk, work in bond_order(rows, "ABCE")
            ]
        else:
            make = functools.partial(advance, step - 1)
            order = bond_order(rows, "BACE")

        def arrive(chunk, step=step):
            if step == 0:
                if chunk == "C":
                    far = [key for key in STATE if key[1][0] != 0]
                    take_state("u", far, u_ref, wide_u)
            elif chunk in ("A", "C"):
                take_late(("f", step - 1), force.at[step - 1], chunk)

        def send(chunk, step=step, name=name, whole=whole):
            ready = {"B": [], "A": ["A", "B"]} if step else {}
            for done in ready.get(chunk, [chunk]):
                send_done(name, CHUNKS, whole, done)

        strain_pass(whole, order, just_in_time(make), arrive, send)
        if step == 0:
            start_all("v", STATE, v_ref)
            take_state("m", STATE, mat_f32, wide_m)
            materials()
        prepare()
        take_sums(name, "sum", whole, sent)
        sent = packed_of(name, "sum", whole)
        if step == 0:
            sent = sent + [("m", STATE, mat_f32), ("v", STATE, v_ref)]

        name = ("f", step)
        whole = force.at[step]
        kind = "final" if last else "crossed"
        run = last_force_pass if last else force_pass
        run(
            whole,
            just_in_time(functools.partial(shift_pressure, step)),
            functools.partial(send_done, name, ORDERS[kind], whole),
        )
        packed_now = packed_of(name, kind, whole)
        take_sums(name, kind, whole, sent + packed_now if last else sent)
        sent = packed_now
        if last:
            mid = pl.ds(REACH, cols)
            for r in range(rows):
                for comp in range(3):
                    pull = force[step, comp, r, mid]
                    speed = wide_v[comp, r, mid] + pull * inertia[r, mid]
                    out_f[comp, r] = pull
                    out_v[comp, r] = speed
                    out_u[comp, r] = wide_u[comp, r, mid] + TIME_STEP * speed


def hand_over(u_in, v_in, f_in, u_out, v_out, f_out):
    u_out[...] = u_in[...]
    v_out[...] = v_in[...]
    f_out[...] = f_in[...]


def on_device(displacement, velocity, intact, material, bulk_modulus, shear_modulus, density):
    rows, cols, nz = material.shape
    wide_rows = rows + REACH
    padded = round_up(cols + 2 * REACH, 8)
    packed = layout(rows, cols)[1]
    own = jax.ShapeDtypeStruct((3, rows, cols, nz), F32)
    vmem = pl.BlockSpec(memory_space=pltpu.VMEM)
    hbm = pl.BlockSpec(memory_space=pltpu.HBM)
    table = pltpu.SMEM(bulk_modulus.shape, F32)

    def buffer(*shape):
        return pltpu.VMEM(shape + (nz,), F32)

    results = pl.pallas_call(
        functools.partial(kernel, lax.axis_size("gx"), lax.axis_size("gy")),
        out_shape=(own, own, own),
        in_specs=[hbm] * 7,
        out_specs=(vmem, vmem, vmem),
        scratch_shapes=[
            buffer(3, rows, cols),
            buffer(3, rows, cols),
            pltpu.VMEM(material.shape, jnp.int32),
            buffer(1, rows, cols),
            table,
            table,
            table,
            pltpu.VMEM(intact.shape, jnp.int32),
            pltpu.VMEM(intact.shape, F32),
            pltpu.VMEM(intact.shape, F32),
            pltpu.VMEM(intact.shape, F32),
            buffer(3, wide_rows, padded),
            buffer(3, wide_rows, padded),
            buffer(1, wide_rows, padded),
            buffer(5, 3, wide_rows, padded),
            buffer(5, wide_rows, padded),
            buffer(5, wide_rows, padded),
            buffer(wide_rows, padded),
            buffer(wide_rows, padded),
            buffer(STEPS, 1, wide_rows, padded),
            buffer(STEPS, 3, wide_rows, padded),
            buffer(packed),
            buffer(packed),
            buffer(3, REACH, cols),
            buffer(1, REACH, cols),
            buffer(3, REACH, cols),
            buffer(STEPS, 2, 1, REACH, padded),
            buffer(STEPS, 2, 3, REACH, padded),
            pltpu.SemaphoreType.DMA((7,)),
            pltpu.SemaphoreType.DMA((len(stages()), SLOTS)),
            pltpu.SemaphoreType.DMA((len(stages()), SLOTS)),
        ],
        compiler_params=pltpu.CompilerParams(
            collective_id=0, has_side_effects=True, vmem_limit_bytes=67_043_328
        ),
        name="peridynamics",
    )(displacement, velocity, intact, material, bulk_modulus, shear_modulus, density)
    return pl.pallas_call(
        hand_over,
        out_shape=(own, own, own),
        in_specs=[vmem] * 3,
        out_specs=(vmem, vmem, vmem),
        name="hand_over",
    )(*results)


def solution(mesh):
    node = P(None, "gx", "gy", None)
    return jax.shard_map(
        on_device,
        mesh=mesh,
        in_specs=(node, node, node, P("gx", "gy", None), P(), P(), P()),
        out_specs=(node, node, node),
        check_vma=False,
    )
```

```python
import functools
import math

import jax
import jax.numpy as jnp
from jax import lax
from jax.experimental import pallas as pl
from jax.experimental.pallas import tpu as pltpu
from jax.sharding import PartitionSpec as P

STEPS = 2
TIME_STEP = 0.02
REACH = 3
NEAR = 2
MESH = pl.DeviceIdType.MESH
F32 = jnp.float32

AROUND = [(dx, dy) for dx in (-1, 0, 1) for dy in (-1, 0, 1) if (dx, dy) != (0, 0)]
STATE = [("S", (-1, 0)), ("S", (0, -1)), ("S", (0, 1)), ("S", (-1, -1)), ("S", (-1, 1))]
CHUNKS = {
    "C": [("C", (1, -1)), ("C", (1, 1)), ("C", (0, -1)), ("C", (0, 1)), ("C", (1, 0))],
    "A": [("A", (-1, -1)), ("A", (-1, 1)), ("A", (0, -1)), ("A", (0, 1)), ("A", (-1, 0))],
    "B": [("B", (0, -1)), ("B", (0, 1))],
    "E": [("E", (0, -1)), ("E", (0, 1))],
}
FINAL = {
    "C": [("C", (1, -1)), ("C", (1, 1)), ("C", (1, 0))],
    "A": [("A", (0, -1)), ("A", (0, 1))],
    "B": [("B", (0, -1)), ("B", (0, 1))],
    "E": [("E", (0, -1)), ("E", (0, 1))],
}
CROSSED = {
    "C": [("C", (1, 0))],
    "A": [("A", (-1, 0))],
    "B": [("B", (0, -1)), ("B", (0, 1))],
    "E": [("E", (0, -1)), ("E", (0, 1))],
    "A late": [("A", (0, -1)), ("A", (0, 1))],
    "C late": [("C", (0, -1)), ("C", (0, 1))],
}
ORDERS = {"sum": CHUNKS, "final": FINAL, "crossed": CROSSED}
SLOT = {key: n for n, key in enumerate(sum(CHUNKS.values(), []))}
SLOTS = len(SLOT)
SLOT.update({key: n for n, key in enumerate(STATE)})


def half_offsets():
    span = range(-REACH, REACH + 1)
    return [
        (a, b, c)
        for a in span
        for b in span
        for c in span
        if a * a + b * b + c * c <= REACH * REACH and (a, b, c) > (0, 0, 0)
    ]


OFFSETS = half_offsets()
GROUPS = {}
for _k, (_a, _b, _c) in enumerate(OFFSETS):
    GROUPS.setdefault((_a, _b), []).append((_k, _c))
RADII = [math.sqrt(float(a * a + b * b + c * c)) for a, b, c in OFFSETS]
VOLUME = 2.0 * sum(RADII)


def round_up(value, unit):
    return -(-value // unit) * unit


AT_PARTNER = [(a, b) for a in (1, 2) for b in (-2, -1, 1, 2)]


def bond_order(rows, order):
    tail = range(rows - REACH, rows)
    groups = list(GROUPS)
    work = {
        "C": [(i, [(a, b) for a, b in groups if i + a >= rows]) for i in tail],
        "A": [(i, groups) for i in range(REACH)],
        "B": [(i, groups) for i in range(REACH, rows - REACH)],
        "E": [(i, [(a, b) for a, b in groups if i + a < rows]) for i in tail],
    }
    return [(chunk, work[chunk]) for chunk in order]


def spans(rows, cols, key, kind):
    chunk, (dx, dy) = key
    own = {(r, c) for r in range(rows) for c in range(cols)}
    wide = own | {(r + a, c + b) for r, c in own for a, b in GROUPS}
    sender = own if kind == "state" else wide
    if kind == "crossed" and dx == 0:
        sender = {(r + x, c) for r, c in wide for x in (-rows, 0, rows)}
    receiver = own if kind == "final" else wide
    if kind == "crossed" and dx != 0:
        receiver = {(r, c + y) for r, c in wide for y in (-cols, 0, cols)}
    first, end = {
        "A": (0, REACH),
        "B": (REACH, rows - REACH),
        "E": (rows - REACH, rows),
        "C": (rows, rows + REACH),
        "S": (0, rows),
    }[chunk]
    runs = []
    for row in range(first, end):
        used = [c for r, c in sender if r == row and (r - dx * rows, c - dy * cols) in receiver]
        if used:
            runs.append((row, min(used), max(used) + 1 - min(used)))
    return runs


def stages():
    listed = [("u", "state", 3), ("m", "state", 1), ("v", "state", 3)]
    for step in range(STEPS):
        listed.append((("t", step), "sum", 1))
        listed.append((("f", step), "final" if step == STEPS - 1 else "crossed", 3))
    return listed


def keys_of(kind):
    if kind == "state":
        return STATE
    return sum(ORDERS[kind].values(), [])


def layout(rows, cols):
    place, at = {}, 0
    for number, (_, kind, comps) in enumerate(stages()):
        for key in keys_of(kind):
            runs = spans(rows, cols, key, kind)
            size = round_up(comps * sum(width for _, _, width in runs), 8)
            place[number, key] = (at, size, runs)
            at += size
    return place, at


def tree_sum(terms):
    while len(terms) > 1:
        terms = [
            terms[n] + terms[n + 1] if n + 1 < len(terms) else terms[n]
            for n in range(0, len(terms), 2)
        ]
    return terms[0]


def kernel(
    grid_rows,
    grid_cols,
    u_hbm,
    v_hbm,
    intact_hbm,
    mat_hbm,
    bulk_hbm,
    shear_hbm,
    dens_hbm,
    out_u,
    out_v,
    out_f,
    u_ref,
    v_ref,
    mat_ref,
    mat_f32,
    bulk_ref,
    shear_ref,
    dens_ref,
    intact_ref,
    flag,
    by_inverse,
    by_stretch,
    wide_u,
    wide_v,
    wide_m,
    u_shift,
    a_shift,
    b_shift,
    a_coef,
    inertia,
    strain,
    force,
    send_buf,
    recv_buf,
    local_sem,
    send_sem,
    recv_sem,
):
    rows, cols, nz = mat_ref.shape
    wide_rows = rows + REACH
    gx = lax.axis_index("gx")
    gy = lax.axis_index("gy")
    place, _ = layout(rows, cols)
    listed = stages()
    number_of = {name: number for number, (name, _, _) in enumerate(listed)}

    def present(direction):
        x = gx + direction[0]
        y = gy + direction[1]
        return (x >= 0) & (x < grid_rows) & (y >= 0) & (y < grid_cols)

    here = {direction: present(direction) for direction in AROUND}

    barrier = pltpu.get_barrier_semaphore()
    for direction in AROUND:

        @pl.when(here[direction])
        def _(direction=direction):
            pl.semaphore_signal(
                barrier,
                inc=1,
                device_id=(gx + direction[0], gy + direction[1]),
                device_id_type=MESH,
            )

    loads = [
        pltpu.make_async_copy(source, target, local_sem.at[n])
        for n, (source, target) in enumerate(
            [
                (u_hbm, u_ref),
                (v_hbm, v_ref),
                (mat_hbm, mat_ref),
                (intact_hbm, intact_ref),
                (bulk_hbm, bulk_ref),
                (shear_hbm, shear_ref),
                (dens_hbm, dens_ref),
            ]
        )
    ]
    for load in loads:
        load.start()

    def copy_to(name, key):
        dx, dy = key[1]
        at, size, _ = place[number_of[name], key]
        return pltpu.make_async_remote_copy(
            src_ref=send_buf.at[at : at + size],
            dst_ref=recv_buf.at[at : at + size],
            send_sem=send_sem.at[number_of[name], SLOT[key]],
            recv_sem=recv_sem.at[number_of[name], SLOT[key]],
            device_id=(gx + dx, gy + dy),
            device_id_type=MESH,
        )

    def pack(name, keys, whole, first_col):
        number = number_of[name]
        comps = listed[number][2]
        for key in keys:
            at, _, runs = place[number, key]
            for comp in range(comps):
                for row, col, width in runs:
                    begin = first_col + col
                    send_buf[at : at + width] = whole[comp, row, begin : begin + width]
                    at += width

    def start_all(name, keys):
        for key in keys:

            @pl.when(here[key[1]])
            def _(key=key):
                copy_to(name, key).start()

    def wait_recv(name, key):
        at, size, _ = place[number_of[name], key]
        target = recv_buf.at[at : at + size]
        pltpu.make_async_remote_copy(
            src_ref=target,
            dst_ref=target,
            send_sem=send_sem.at[number_of[name], SLOT[key]],
            recv_sem=recv_sem.at[number_of[name], SLOT[key]],
            device_id=(gx - key[1][0], gy - key[1][1]),
            device_id_type=MESH,
        ).wait_recv()

    def wait_sends(name, keys):
        for key in keys:

            @pl.when(here[key[1]])
            def _(key=key):
                copy_to(name, key).wait_send()

    def landed(name, key):
        number = number_of[name]
        at, _, runs = place[number, key]
        dx, dy = key[1]
        for comp in range(listed[number][2]):
            for row, col, width in runs:
                yield comp, row - dx * rows, REACH + col - dy * cols, at, width
                at += width

    def take_state(name, keys, wide):
        for key in keys:
            origin = (-key[1][0], -key[1][1])

            @pl.when(here[origin])
            def _(key=key):
                wait_recv(name, key)
                for comp, row, col, at, width in landed(name, key):
                    wide[comp, row, col : col + width] = recv_buf[at : at + width]

    def take_sum(name, key, whole):
        origin = (-key[1][0], -key[1][1])

        @pl.when(here[origin])
        def _():
            wait_recv(name, key)
            for comp, row, col, at, width in landed(name, key):
                span = slice(col, col + width)
                whole[comp, row, span] = whole[comp, row, span] + recv_buf[at : at + width]

    def take_sums(name, kind, whole, sent):
        order = ORDERS[kind]
        if kind == "crossed":
            for key, late in ((order["C"][0], "A late"), (order["A"][0], "C late")):
                take_sum(name, key, whole)
                send_done(name, order, whole, late)
        else:
            for key in order["C"] + order["A"]:
                take_sum(name, key, whole)
        for other in sent:
            wait_sends(*other)
        if name == ("f", 0):
            take_state("v", STATE, wide_v)
        for key in order["B"] + order["E"]:
            take_sum(name, key, whole)

    def take_late(name, whole, chunk):
        for key in CROSSED[chunk + " late"]:
            take_sum(name, key, whole)

    loads[0].wait()
    pack("u", STATE, u_ref, 0)
    loads[2].wait()
    mat_f32[0] = mat_ref[...].astype(F32)
    pack("m", STATE, mat_f32, 0)

    on_x = (gx > 0).astype(jnp.int32) + (gx < grid_rows - 1).astype(jnp.int32)
    on_y = (gy > 0).astype(jnp.int32) + (gy < grid_cols - 1).astype(jnp.int32)
    pl.semaphore_wait(barrier, (1 + on_x) * (1 + on_y) - 1)
    start_all("u", STATE)

    loads[1].wait()
    pack("v", STATE, v_ref, 0)

    wide_u[...] = jnp.zeros(wide_u.shape, F32)
    wide_v[...] = jnp.zeros(wide_v.shape, F32)
    wide_m[...] = jnp.zeros(wide_m.shape, F32)
    for comp in range(3):
        wide_u[comp, 0:rows, REACH : REACH + cols] = u_ref[comp]
        wide_v[comp, 0:rows, REACH : REACH + cols] = v_ref[comp]
    wide_m[0, 0:rows, REACH : REACH + cols] = mat_f32[0]

    def shifted(values, c):
        if c == 0:
            return values
        lane = lax.broadcasted_iota(jnp.int32, values.shape, 1)
        moved = pltpu.roll(values, (-c) % nz, axis=1)
        return jnp.where((lane + c >= 0) & (lane + c < nz), moved, 0.0)

    def shifts(r):
        return (0,) if r == wide_rows - 1 else range(-NEAR, NEAR + 1)

    def shift_motion(r):
        for comp in range(3):
            values = wide_u[comp, r]
            for c in shifts(r):
                moved = shifted(values, c)
                if comp == 2 and c != 0:
                    moved = moved + float(c)
                u_shift[c + NEAR, comp, r] = moved

    def advance(step, r):
        for comp in range(3):
            speed = wide_v[comp, r] + force[step, comp, r] * inertia[r]
            wide_v[comp, r] = speed
            wide_u[comp, r] = wide_u[comp, r] + TIME_STEP * speed
        shift_motion(r)

    def shift_pressure(step, r):
        values = strain[step, 0, r] * a_coef[r]
        for c in shifts(r):
            a_shift[c + NEAR, r] = shifted(values, c)

    def just_in_time(make):
        made = set()

        def need(i, groups):
            for r in sorted({i} | {i + a for a, _ in groups}):
                if r not in made:
                    made.add(r)
                    make(r)

        return need

    def materials():
        for r in range(wide_rows):
            classes = wide_m[0, r]
            bulk = jnp.full(classes.shape, bulk_ref[0], F32)
            shear = jnp.full(classes.shape, shear_ref[0], F32)
            dens = jnp.full(classes.shape, dens_ref[0], F32)
            for number in range(1, bulk_ref.shape[0]):
                match = classes == float(number)
                bulk = jnp.where(match, bulk_ref[number], bulk)
                shear = jnp.where(match, shear_ref[number], shear)
                dens = jnp.where(match, dens_ref[number], dens)
            inertia[r] = TIME_STEP / dens
            a_coef[r] = (9.0 / (VOLUME * VOLUME)) * (bulk - (5.0 / 3.0) * shear)
            stiff = (15.0 / VOLUME) * shear
            for c in shifts(r):
                b_shift[c + NEAR, r] = shifted(stiff, c)

    depth = lax.broadcasted_iota(jnp.int32, (cols, nz), 1)
    column = lax.broadcasted_iota(jnp.int32, (cols, nz), 0) + gy * cols

    def partner(buffer, i, a, b, c, own):
        if c > NEAR:
            return shifted(own, c)
        return buffer[c + NEAR, i + a, pl.ds(REACH + b, cols)]

    def bond_vector(i, a, b, c, own):
        y = []
        for comp in range(3):
            if c > NEAR:
                there = shifted(own[3][comp], c)
                if comp == 2:
                    there = there + float(c)
            else:
                there = u_shift[c + NEAR, comp, i + a, pl.ds(REACH + b, cols)]
            y.append(there - (own[0][a], own[1][b], own[2])[comp])
        return y

    def geometry(i, a, b, c, own):
        y0, y1, y2 = bond_vector(i, a, b, c, own)
        square = y0 * y0 + y1 * y1 + y2 * y2
        inverse = lax.rsqrt(square)
        return square * inverse, inverse

    def own_motion(i):
        mine = [wide_u[comp, i, REACH : REACH + cols] for comp in range(3)]
        by_row = {a: mine[0] - float(a) for a in range(REACH + 1)}
        by_col = {b: mine[1] - float(b) for b in range(-REACH, REACH + 1)}
        return (by_row, by_col, mine[2], mine)

    def back(values, c):
        return values if c == 0 else pltpu.roll(values, c % nz, axis=1)

    def send_done(name, keys, whole, chunk):
        pack(name, keys[chunk], whole, REACH)
        start_all(name, keys[chunk])

    def weights():
        @pl.loop(0, rows)
        def _(i):
            lane_in = {
                c: jnp.where((depth + c >= 0) & (depth + c < nz), 1.0, 0.0)
                for c in range(-NEAR, REACH + 1)
            }
            for (a, b), members in GROUPS.items():
                row_in = (gx * rows + i + a) < grid_rows * rows
                plane = jnp.where(
                    (column + b >= 0) & (column + b < grid_cols * cols) & row_in, 1.0, 0.0
                )
                for k, c in members:
                    flag[k, i] = intact_ref[k, i].astype(F32) * (plane * lane_in[c])

    def prepare():
        @pl.loop(0, rows)
        def _(i):
            own_b = b_shift[NEAR, i, pl.ds(REACH, cols)]
            for k, (a, b, c) in enumerate(OFFSETS):
                both_b = own_b + partner(b_shift, i, a, b, c, own_b)
                scale = flag[k, i] * by_inverse[k, i]
                by_stretch[k, i] = scale * (both_b * (by_stretch[k, i] * (1.0 / RADII[k])))
                by_inverse[k, i] = scale

    def stays(i, a, b):
        return b == 0 and i + a < rows

    def strain_pass(sums_ref, order, need, arrive, send):
        mid = pl.ds(REACH, cols)
        for chunk, work in order:
            arrive(chunk)
            for i, groups in work:
                need(i, groups)
                own = own_motion(i)
                sums = []
                for a, b in groups:
                    returned = []
                    for k, c in GROUPS[a, b]:
                        length, inverse = geometry(i, a, b, c, own)
                        stretch = length - RADII[k]
                        by_inverse[k, i] = inverse
                        by_stretch[k, i] = stretch
                        term = flag[k, i] * stretch
                        sums.append(term)
                        returned.append(back(term, c))
                    at = pl.ds(REACH + b, cols)
                    sums_ref[0, i + a, at] = sums_ref[0, i + a, at] + tree_sum(returned)
                    sums = [tree_sum(sums)]
                sums_ref[0, i, mid] = sums_ref[0, i, mid] + sums[0]
            send(chunk)

    def tensions_of(i, a, b, own_a):
        found = []
        for k, c in GROUPS[a, b]:
            both_a = own_a + partner(a_shift, i, a, b, c, own_a)
            found.append((c, by_inverse[k, i] * both_a + by_stretch[k, i]))
        return found

    def pull_origin(i, a, b, tensions, own):
        at = pl.ds(REACH + b, cols)
        base = (own[0][a], own[1][b], own[2])
        total = tree_sum([tension for _, tension in tensions])
        return [
            tree_sum([t * u_shift[c + NEAR, comp, i + a, at] for c, t in tensions])
            - base[comp] * total
            for comp in range(3)
        ]

    def pull_partner(i, a, b, tensions, sums_ref):
        mid = pl.ds(REACH, cols)
        at = pl.ds(REACH + b, cols)
        pulled = [(c, back(tension, c)) for c, tension in tensions]
        total = tree_sum([tension for _, tension in pulled])
        for comp, shift in enumerate((float(a), float(b), 0.0)):
            origin = tree_sum([t * u_shift[NEAR - c, comp, i, mid] for c, t in pulled])
            end = u_shift[NEAR, comp, i + a, at] + shift
            sums_ref[comp, i + a, at] = sums_ref[comp, i + a, at] + (origin - end * total)

    def pull_both(i, a, b, tensions, own, sums_ref, sums):
        at = pl.ds(REACH + b, cols)
        returned = [[], [], []]
        for c, tension in tensions:
            y = bond_vector(i, a, b, c, own)
            for comp in range(3):
                term = tension * y[comp]
                sums[comp].append(term)
                returned[comp].append(back(term, c))
        for comp in range(3):
            sums_ref[comp, i + a, at] = sums_ref[comp, i + a, at] - tree_sum(returned[comp])

    def force_pass(sums_ref, need, send):
        mid = pl.ds(REACH, cols)
        for chunk, work in bond_order(rows, "CABE"):
            for i, groups in work:
                need(i, groups)
                own = own_motion(i)
                own_a = a_shift[NEAR, i, mid]
                sums = [[], [], []]
                for a, b in groups:
                    tensions = tensions_of(i, a, b, own_a)
                    if (a, b) in AT_PARTNER:
                        for comp, part in enumerate(pull_origin(i, a, b, tensions, own)):
                            sums[comp].append(part)
                        pull_partner(i, a, b, tensions, sums_ref)
                    else:
                        pull_both(i, a, b, tensions, own, sums_ref, sums)
                    sums = [[tree_sum(sums[comp])] for comp in range(3)]
                for comp in range(3):
                    sums_ref[comp, i, mid] = sums_ref[comp, i, mid] + sums[comp][0]
            send(chunk)

    def last_force_pass(sums_ref, need, send):
        mid = pl.ds(REACH, cols)
        for chunk, work in bond_order(rows, "CABE"):
            for i, groups in work:
                leaving = [(a, b) for a, b in groups if b != 0 or i + a >= rows]
                need(i, groups)
                own_a = a_shift[NEAR, i, mid]
                for a, b in leaving:
                    tensions = tensions_of(i, a, b, own_a)
                    for (k, _), (_, tension) in zip(GROUPS[a, b], tensions):
                        by_stretch[k, i] = tension
                    pull_partner(i, a, b, tensions, sums_ref)
            send(chunk)
        for i in range(rows):
            own = own_motion(i)
            own_a = a_shift[NEAR, i, mid]
            sums = [[], [], []]
            for a, b in GROUPS:
                if b != 0 or i + a >= rows:
                    tensions = [(c, by_stretch[k, i]) for k, c in GROUPS[a, b]]
                    for comp, part in enumerate(pull_origin(i, a, b, tensions, own)):
                        sums[comp].append(part)
                else:
                    tensions = tensions_of(i, a, b, own_a)
                    pull_both(i, a, b, tensions, own, sums_ref, sums)
                sums = [[tree_sum(sums[comp])] for comp in range(3)]
            for comp in range(3):
                sums_ref[comp, i, mid] = sums_ref[comp, i, mid] + sums[comp][0]

    for load in loads[3:]:
        load.wait()
    weights()
    strain[...] = jnp.zeros(strain.shape, F32)
    force[...] = jnp.zeros(force.shape, F32)
    start_all("m", STATE)

    def near(i, groups):
        return [(a, b) for a, b in groups if stays(i, a, b)]

    def rest(i, groups):
        return [(a, b) for a, b in groups if not stays(i, a, b)]

    strain_pass(
        strain.at[0],
        [("", [(i, near(i, GROUPS)) for i in range(rows)])],
        just_in_time(shift_motion),
        lambda chunk: None,
        lambda chunk: None,
    )
    take_state("u", [key for key in STATE if key[1][0] == 0], wide_u)

    sent = [("u", STATE)]
    for step in range(STEPS):
        last = step == STEPS - 1
        name = ("t", step)
        whole = strain.at[step]
        if step == 0:
            make = shift_motion
            order = [
                (chunk, [(i, rest(i, groups)) for i, groups in work])
                for chunk, work in bond_order(rows, "ABCE")
            ]
        else:
            make = functools.partial(advance, step - 1)
            order = bond_order(rows, "BACE")

        def arrive(chunk, step=step):
            if step == 0:
                if chunk == "C":
                    far = [key for key in STATE if key[1][0] != 0]
                    take_state("u", far, wide_u)
            elif chunk in ("A", "C"):
                take_late(("f", step - 1), force.at[step - 1], chunk)

        def send(chunk, step=step, name=name, whole=whole):
            ready = {"B": [], "A": ["A", "B"]} if step else {}
            for done in ready.get(chunk, [chunk]):
                send_done(name, CHUNKS, whole, done)

        strain_pass(whole, order, just_in_time(make), arrive, send)
        if step == 0:
            start_all("v", STATE)
            take_state("m", STATE, wide_m)
            materials()
        prepare()
        take_sums(name, "sum", whole, sent)
        sent = [(name, keys_of("sum"))]
        if step == 0:
            sent = sent + [("m", STATE), ("v", STATE)]

        name = ("f", step)
        whole = force.at[step]
        kind = "final" if last else "crossed"
        run = last_force_pass if last else force_pass
        run(
            whole,
            just_in_time(functools.partial(shift_pressure, step)),
            functools.partial(send_done, name, ORDERS[kind], whole),
        )
        packed_now = [(name, keys_of(kind))]
        take_sums(name, kind, whole, sent + packed_now if last else sent)
        sent = packed_now
        if last:
            mid = pl.ds(REACH, cols)
            for r in range(rows):
                for comp in range(3):
                    pull = force[step, comp, r, mid]
                    speed = wide_v[comp, r, mid] + pull * inertia[r, mid]
                    out_f[comp, r] = pull
                    out_v[comp, r] = speed
                    out_u[comp, r] = wide_u[comp, r, mid] + TIME_STEP * speed


def hand_over(u_in, v_in, f_in, u_out, v_out, f_out):
    u_out[...] = u_in[...]
    v_out[...] = v_in[...]
    f_out[...] = f_in[...]


def on_device(displacement, velocity, intact, material, bulk_modulus, shear_modulus, density):
    rows, cols, nz = material.shape
    wide_rows = rows + REACH
    padded = round_up(cols + 2 * REACH, 8)
    packed = layout(rows, cols)[1]
    own = jax.ShapeDtypeStruct((3, rows, cols, nz), F32)
    vmem = pl.BlockSpec(memory_space=pltpu.VMEM)
    hbm = pl.BlockSpec(memory_space=pltpu.HBM)
    table = pltpu.SMEM(bulk_modulus.shape, F32)

    def buffer(*shape):
        return pltpu.VMEM(shape + (nz,), F32)

    results = pl.pallas_call(
        functools.partial(kernel, lax.axis_size("gx"), lax.axis_size("gy")),
        out_shape=(own, own, own),
        in_specs=[hbm] * 7,
        out_specs=(vmem, vmem, vmem),
        scratch_shapes=[
            buffer(3, rows, cols),
            buffer(3, rows, cols),
            pltpu.VMEM(material.shape, jnp.int32),
            buffer(1, rows, cols),
            table,
            table,
            table,
            pltpu.VMEM(intact.shape, jnp.int32),
            pltpu.VMEM(intact.shape, F32),
            pltpu.VMEM(intact.shape, F32),
            pltpu.VMEM(intact.shape, F32),
            buffer(3, wide_rows, padded),
            buffer(3, wide_rows, padded),
            buffer(1, wide_rows, padded),
            buffer(5, 3, wide_rows, padded),
            buffer(5, wide_rows, padded),
            buffer(5, wide_rows, padded),
            buffer(wide_rows, padded),
            buffer(wide_rows, padded),
            buffer(STEPS, 1, wide_rows, padded),
            buffer(STEPS, 3, wide_rows, padded),
            buffer(packed),
            buffer(packed),
            pltpu.SemaphoreType.DMA((7,)),
            pltpu.SemaphoreType.DMA((len(stages()), SLOTS)),
            pltpu.SemaphoreType.DMA((len(stages()), SLOTS)),
        ],
        compiler_params=pltpu.CompilerParams(
            collective_id=0, has_side_effects=True, vmem_limit_bytes=67_043_328
        ),
        name="peridynamics",
    )(displacement, velocity, intact, material, bulk_modulus, shear_modulus, density)
    return pl.pallas_call(
        hand_over,
        out_shape=(own, own, own),
        in_specs=[vmem] * 3,
        out_specs=(vmem, vmem, vmem),
        name="hand_over",
    )(*results)


def solution(mesh):
    node = P(None, "gx", "gy", None)
    return jax.shard_map(
        on_device,
        mesh=mesh,
        in_specs=(node, node, node, P("gx", "gy", None), P(), P(), P()),
        out_specs=(node, node, node),
        check_vma=False,
    )
```
